32 devices in a mesh: chan: 4 (over y, x), hid: 8 (over z, core).
Axes of the slice: x: 2, y: 2, z: 4, core: 2. Of those that a mesh axis runs over, the one named last changes fastest.
Arguments:
- pixels: bfloat16 [384, 256, 256], P('chan'), may hold values from -6 to 6
- patch_weight: bfloat16 [384, 256, 6144], P('chan', None, 'hid'), may hold values from -0.375 to 0.375
- channel_embed: bfloat16 [384, 6144], P('chan', 'hid'), may hold values from -3 to 3
- pool_query: bfloat16 [48, 6144], P('chan', 'hid'), may hold values from -2.5 to 2.5
- group_mix: bfloat16 [48, 6144], P('chan', 'hid'), may hold values from -3.2 to 3.2
- assign: int32 [384], P('chan'), may hold values from 0 to 47, as said below
- ln_gain: float32 [6144], P('chan'), may hold values from 0.1 to 1.9
- w_qkv: bfloat16 [6144, 3, 6144], P('chan', None, 'hid'), may hold values from -0.078125 to 0.078125
- w_up: bfloat16 [6144, 24576], P('chan', 'hid'), may hold values from -0.078125 to 0.078125
- b_up: float32 [24576], P('hid'), may hold values from -3 to 3
- w_out: bfloat16 [6144, 6144], P('hid', 'chan'), may hold values from -0.078125 to 0.078125
- w_down: bfloat16 [24576, 6144], P('hid', 'chan'), may hold values from -0.0390625 to 0.0390625
Outputs:
- block_out: bfloat16 [256, 6144], P(None, 'chan')
The draws below stay inside these ranges and needn't reach their ends.
Inputs may be any that keep to these rules, and one draw needn't show every extreme that they name: Channel c belongs to group assign[c]; every group holds exactly 8 channels, and group k's channels all lie among the 96 consecutive channels beginning at channel (k // 12) * 96.
All inputs are finite; a program needn't handle non-finite values.
Results may differ from the reference program's by a relative error of at most 0.02.
Values may be sent and summed in bfloat16 or wider, within the bound.
A program may use at most 320 MiB of HBM per device.

```python
import math
import jax
import jax.numpy as jnp
from jax import lax

HS = 128
HEADS = 48
FF = 24576
C = 384
G = 48
P2 = 256
PATCHES = 256
IMAGES = 1
D = 6144
TOKENS = 256
CH_DEV = 96
G_DEV = 12


def draw_assign(key, part):
    blocks = C // CH_DEV
    raw_keys = jax.random.randint(key, (C,), 0, 1 << 20, dtype=jnp.int32) * C + jnp.arange(C, dtype=jnp.int32)
    row_keys = raw_keys.reshape(blocks, CH_DEV)
    rankings = jnp.argsort(jnp.argsort(row_keys, axis=1), axis=1).astype(jnp.int32)
    groups = jnp.arange(blocks, dtype=jnp.int32)[:, None] * G_DEV + rankings // (C // G)
    return groups.reshape(C).astype(jnp.int32)


def draw_group_mix(key, part):
    columns = jnp.arange(D, dtype=jnp.float32) / D
    base = jnp.clip(jax.random.normal(key, (G, D), jnp.float32), -4.0, 4.0)
    ramp = 0.08 * jnp.exp(math.log(10.0) * columns)
    return (base * ramp[None, :]).astype(jnp.bfloat16)


def shard_levels(stream_key, extent, shards, low, top_value):
    def one(dim, parts):
        steps = jax.random.uniform(jax.random.fold_in(jax.random.fold_in(stream_key, 6), dim), (parts,), jnp.float32, low / len(shards), top_value / len(shards))
        return jnp.repeat(jnp.exp(steps), extent[dim] // parts).reshape((-1,) + (1,) * (len(extent) - dim - 1))

    gain = one(*shards[0])
    for cut in shards[1:]:
        gain = gain * one(*cut)
    return gain


def scatter_about(key, shape, spread, bound, cuts=(), held_as=jnp.bfloat16):
    values = jax.random.normal(key, shape, jnp.float32) * spread
    if len(cuts) > 0:
        values = shard_levels(key, shape, cuts, -0.22, 0.18) * values
    return jnp.clip(values, min=-bound, max=bound).astype(held_as)


def setup_inputs(seed: int = 0) -> dict:
    seeds = jax.random.split(jax.random.key(seed), 13)
    pixels = scatter_about(seeds[0], (C, TOKENS, P2), 1.0, 6.0, ((0, 4),))
    patch_weight = scatter_about(seeds[1], (C, P2, D), P2 ** -0.5, 0.375, ((0, 4), (2, 8)))
    channel_embed = scatter_about(seeds[2], (C, D), 0.5, 3.0, ((0, 4), (1, 8)))
    pool_query = scatter_about(seeds[3], (G, D), 1.0, 2.5, ((0, 4), (1, 8)))
    group_mix = draw_group_mix(jax.random.fold_in(seeds[12], 71), 0)
    assign = draw_assign(jax.random.fold_in(seeds[12], 71), 0)
    ln_gain = jnp.clip(1.0 + 0.18 * jax.random.normal(seeds[6], (D,), jnp.float32), 0.1, 1.9)
    w_qkv = scatter_about(seeds[7], (D, 3, D), D ** -0.5, 0.078125, ((0, 4), (2, 8)))
    w_up = scatter_about(seeds[8], (D, FF), D ** -0.5, 0.078125, ((0, 4), (1, 8)))
    b_up = scatter_about(seeds[9], (FF,), 0.5, 3.0, ((0, 8),), jnp.float32)
    w_out = scatter_about(seeds[10], (D, D), D ** -0.5, 0.078125, ((0, 8), (1, 4)))
    w_down = scatter_about(seeds[11], (FF, D), FF ** -0.5, 0.0390625, ((0, 8), (1, 4)))
    return {"pixels": pixels, "patch_weight": patch_weight, "channel_embed": channel_embed, "pool_query": pool_query, "group_mix": group_mix, "assign": assign, "ln_gain": ln_gain, "w_qkv": w_qkv, "w_up": w_up, "b_up": b_up, "w_out": w_out, "w_down": w_down}


epsilon = 1e-06

def head_norm(values):
    return values * lax.rsqrt(lax.optimization_barrier(jnp.mean(values * values, axis=-1, keepdims=True)) + epsilon)

def reference(pixels, patch_weight, channel_embed, pool_query, group_mix, assign, ln_gain, w_qkv, w_up, b_up, w_out, w_down):
    group_size = C // G
    ordering = jnp.argsort(assign, stable=True).astype(jnp.int32).reshape(G, group_size)

    def add_group(carry, group_idx):
        members = ordering[group_idx]
        patches = pixels[members].astype(jnp.float32)
        weights = patch_weight[members].astype(jnp.float32)
        embedded = jnp.einsum('ctp,cpd->ctd', patches, weights, precision=lax.Precision.HIGHEST)
        embedded = embedded + channel_embed[members].astype(jnp.float32)[:, None, :]
        features = jax.nn.gelu(embedded, approximate=False)
        split = features.reshape(group_size, TOKENS, HEADS, HS)
        normed = head_norm(split)
        query = pool_query[group_idx].astype(jnp.float32).reshape(HEADS, HS)
        score = jnp.einsum('cthe,he->cth', normed, query, precision=lax.Precision.HIGHEST) / math.sqrt(HS)
        shift = jnp.sqrt(lax.optimization_barrier(jnp.sum(query * query, axis=-1)))
        weight = jnp.exp(score - shift)
        numer = lax.optimization_barrier(jnp.sum(weight[..., None] * split, axis=0))
        denom = lax.optimization_barrier(jnp.sum(weight, axis=0))
        pooled = (numer / denom[..., None]).reshape(TOKENS, D)
        return (carry + pooled * group_mix[group_idx].astype(jnp.float32), None)
    result = lax.scan(add_group, jnp.zeros((TOKENS, D), jnp.float32), jnp.arange(G, dtype=jnp.int32))
    layer_input = result[0].astype(jnp.bfloat16)
    wide = layer_input.astype(jnp.float32)
    row_mean = lax.optimization_barrier(jnp.sum(wide, axis=1)) / D
    row_var = lax.optimization_barrier(jnp.sum(wide * wide, axis=1)) / D - row_mean * row_mean
    normed_input = ((wide - row_mean[:, None]) * lax.rsqrt(row_var + epsilon)[:, None] * ln_gain).astype(jnp.bfloat16)
    qkv_sum = jnp.dot(normed_input, w_qkv.reshape(D, 3 * D), preferred_element_type=jnp.float32)
    up_sum = jnp.dot(normed_input, w_up, preferred_element_type=jnp.float32) + b_up
    heads = qkv_sum.reshape(IMAGES, PATCHES, 3, HEADS, HS)
    queries = head_norm(heads[:, :, 0]).astype(jnp.bfloat16)
    keys = head_norm(heads[:, :, 1]).astype(jnp.bfloat16)
    values = heads[:, :, 2].astype(jnp.bfloat16)
    scores = jnp.einsum('bqhe,bkhe->bhqk', queries.astype(jnp.float32), keys.astype(jnp.float32)) * (2.0 / math.sqrt(HS))
    expo = jnp.exp(scores)
    probs = (expo / lax.optimization_barrier(jnp.sum(expo, axis=-1, keepdims=True))).astype(jnp.bfloat16)
    attended = jnp.einsum('bhqk,bkhe->bqhe', probs.astype(jnp.float32), values.astype(jnp.float32))
    attended = attended.astype(jnp.bfloat16).reshape(TOKENS, D)
    hidden = jax.nn.gelu(up_sum, approximate=False).astype(jnp.bfloat16)
    mixed = jnp.dot(attended, w_out, preferred_element_type=jnp.float32) + jnp.dot(hidden, w_down, preferred_element_type=jnp.float32)
    return (wide + mixed).astype(jnp.bfloat16)
```

```python
import functools
import math

import jax
import jax.numpy as jnp
from jax import lax
from jax.experimental import pallas as pl
from jax.experimental.pallas import tpu as pltpu
from jax.sharding import PartitionSpec as P

HS = 128
PATCHES = 256


epsilon = 1e-06


ACROSS = (((1,), (1,)), ((), ()))
LOG2E = math.log2(math.e)
SLOT = 16
ROWS = 256
CPS = 4


def pool_setup(groups, size, query, mix, emb, quer, pick, shift, mixs, embs, fan):
    width = quer.shape[1]
    own = lax.broadcasted_iota(jnp.int32, (SLOT, width), 0) == lax.broadcasted_iota(jnp.int32, (SLOT, width), 1) // HS
    q = query[...].astype(jnp.float32)
    m = mix[...].astype(jnp.float32) * math.sqrt(0.5)
    pick[...] = jnp.where(own, 1.0, 0.0).astype(jnp.bfloat16)
    for g in range(groups):
        row = jnp.where(own, q[g:g+1, :], 0.0)
        rs = slice(g*SLOT, (g+1)*SLOT)
        quer[rs, :] = row.astype(jnp.bfloat16)
        n = jnp.sqrt(jnp.sum(row * row, axis=1, keepdims=True)) * LOG2E
        shift[rs, :] = jnp.broadcast_to(n, (SLOT, HS))
        mixs[g] = m[g:g+1]
    for c in range(0, emb.shape[0], 8):
        e = emb[c:c+8, :].astype(jnp.float32) * math.sqrt(0.5)
        for k in range(8):
            embs[c+k] = e[k:k+1]
    kind = lax.rem(lax.broadcasted_iota(jnp.int32, (HS, width), 0), HS // 2)
    head = lax.broadcasted_iota(jnp.int32, (HS, width), 1) // HS
    for j in range(size):
        fan[j] = jnp.where(kind == j * 8 + head, 1.0, 0.0).astype(jnp.bfloat16)

def features(tok, px_of, pw_of, bias, put):
    width = bias.shape[1]
    step = min(256, width)
    R = min(ROWS, tok)
    for n in range(width // step):
        cs = slice(n*step, (n+1)*step)
        for r in range(0, tok, R):
            e = jnp.dot(px_of(r, R), pw_of(cs), preferred_element_type=jnp.float32)
            u = e * math.sqrt(0.5) + bias[:, cs]
            g = (u * (1.0 + lax.erf(u))).astype(jnp.bfloat16)
            put(r, R, cs, g, g * g)

def weigh(tok, g, s, local, quer, pick, shift):
    rs = pl.ds(pl.multiple_of(local * SLOT, SLOT), SLOT)
    dots = lax.dot_general(quer[rs, :], g[...], ACROSS, preferred_element_type=jnp.float32)
    total = lax.dot_general(pick[...], s[...], ACROSS, preferred_element_type=jnp.float32)
    sh = jnp.concatenate([shift[rs, :]] * (tok // HS), axis=1)
    score = dots * lax.rsqrt(total * (1.0 / HS) + 2 * epsilon) * (LOG2E / math.sqrt(HS))
    return jnp.exp2(score - sh)[0:8, :]

def merge(groups, size, tok, order, feat, wts, mixs, fan, acc):
    width = feat.shape[2]
    step = min(256, width)
    def group(g, _):
        cs = [order[g*size + j] for j in range(size)]
        for b in range(0, tok, HS):
            bs = slice(b, b + HS)
            ws = [wts[c, :, bs] for c in cs]
            den = ws[0]
            for w in ws[1:]:
                den = den + w
            inv = 1.0 / den
            w = jnp.concatenate([w * inv for w in ws], axis=0)
            hi = w.astype(jnp.bfloat16).astype(jnp.float32)
            both = jnp.transpose(jnp.concatenate([hi, w - hi], axis=0))
            lhs = both.astype(jnp.bfloat16)
            for n in range(width // step):
                ns = slice(n*step, (n+1)*step)
                p = None
                for j in range(size):
                    t = jnp.dot(lhs, fan[j, :, ns], preferred_element_type=jnp.float32) * feat[cs[j], bs, ns].astype(jnp.float32)
                    p = t if p is None else p + t
                acc[bs, ns] += p * mixs[g, :, ns]
        return 0
    lax.fori_loop(0, groups, group, 0)

def pool_kernel(groups, size, order, assign, pix, pw, emb, query, mix, out, feat, wts, acc, quer, pick, shift, mixs, embs, fan, g0, g1, s0, s1):
    t = pl.program_id(0); c = pl.program_id(1)
    tok = out.shape[0]
    gb, sb = (g0, g1), (s0, s1)
    @pl.when((t == 0) & (c == 0))
    def _():
        pool_setup(groups, size, query, mix, emb, quer, pick, shift, mixs, embs, fan)
    @pl.when(c == 0)
    def _():
        acc[...] = jnp.zeros_like(acc)
    def back(k):
        cc = c * CPS + k
        wts[cc] = weigh(tok, gb[k % 2], sb[k % 2], lax.rem(assign[cc], groups), quer, pick, shift)
    for k in range(CPS):
        cc = c * CPS + k
        def put(r, R, cs, g, s):
            feat[cc, r:r+R, cs] = g
            gb[k % 2][r:r+R, cs] = g
            sb[k % 2][r:r+R, cs] = s
        features(tok, lambda r, R: pix[k, r:r+R, :], lambda cs: pw[k, :, cs], embs[cc], put)
        if k: back(k - 1)
    back(CPS - 1)
    @pl.when(c == pl.num_programs(1)-1)
    def _():
        merge(groups, size, tok, order, feat, wts, mixs, fan, acc)
        out[...] = acc[...].astype(jnp.bfloat16)

def pool(T, pixels, patch_weight, channel_embed, pool_query, group_mix, assign):
    chans, tok, p2 = pixels.shape
    width = patch_weight.shape[2]
    groups = pool_query.shape[0]
    size = chans // groups
    idx = jnp.arange(chans, dtype=jnp.int32)
    key = assign * chans + idx
    rank = jnp.sum((key[None, :] < key[:, None]).astype(jnp.int32), axis=1)
    order = jnp.sum(jnp.where(rank[None, :] == idx[:, None], idx[None, :], 0), axis=1).astype(jnp.int32)
    full = lambda s: pl.BlockSpec(s, lambda t, c, *_: (0,)*len(s))
    vm = pltpu.VMEM
    spec = pltpu.PrefetchScalarGridSpec(num_scalar_prefetch=2, grid=(tok//T, chans//CPS),
        in_specs=[pl.BlockSpec((CPS,T,p2), lambda t,c,*_:(c,t,0)), pl.BlockSpec((CPS,p2,width), lambda t,c,*_:(c,0,0)),
          full((chans,width)), full((groups,width)), full((groups,width))],
        out_specs=pl.BlockSpec((T,width), lambda t,c,*_:(t,0)),
        scratch_shapes=[vm((chans,T,width), jnp.bfloat16), vm((chans,8,T), jnp.float32),
          vm((T,width), jnp.float32), vm((groups*SLOT,width), jnp.bfloat16), vm((SLOT,width), jnp.bfloat16),
          vm((groups*SLOT,HS), jnp.float32), vm((groups,1,width), jnp.float32), vm((chans,1,width), jnp.float32),
          vm((size,HS,width), jnp.bfloat16)] + [vm((T,width), jnp.bfloat16)]*4)
    return pl.pallas_call(functools.partial(pool_kernel, groups, size), grid_spec=spec, out_shape=jax.ShapeDtypeStruct((tok,width), jnp.bfloat16),
        compiler_params=pltpu.CompilerParams(dimension_semantics=("arbitrary","arbitrary"), vmem_limit_bytes=62<<20), name="pool")(
        order, assign, pixels, patch_weight, channel_embed, pool_query, group_mix)
def head_norm(values):
    return values * lax.rsqrt(jnp.mean(values * values, axis=-1, keepdims=True) + epsilon)


MESH = pl.DeviceIdType.MESH


def greet(peers):
    gate = pltpu.get_barrier_semaphore()
    for peer in peers:
        pl.semaphore_signal(gate, inc=1, device_id=peer, device_id_type=MESH)
    pl.semaphore_wait(gate, len(peers))


def send(src, dst, sems, slot, peer):
    copy = pltpu.make_async_remote_copy(
        src_ref=src, dst_ref=dst, send_sem=sems.at[0, slot], recv_sem=sems.at[1, slot],
        device_id=peer, device_id_type=MESH)
    copy.start()
    return copy


def places(chans, hids):
    a, b = lax.axis_index("chan"), lax.axis_index("hid")
    chips, chip, core = hids // 2, b // 2, b % 2
    rows = [{"chan": lax.rem(a + k, chans)} for k in range(1, chans)]
    far = [{"hid": lax.rem(chip + k, chips) * 2 + core} for k in range(1, chips)]
    return a, b, chips, chip, core, rows, far, {"hid": chip * 2 + (1 - core)}


def spread(src_of, slots, chips, chip, core, far, mate, away, near):
    sent = [send(src_of(chip * 2 + core), src_of(chip * 2 + core), away, k, peer) for k, peer in enumerate(far)]
    mine = src_of(chip * 2 + core)
    passed = [send(mine, mine, near, 0, mate)]
    for k in range(1, chips):
        sent[k - 1].wait_recv()
        piece = src_of(lax.rem(chip + chips - k, chips) * 2 + core)
        passed.append(send(piece, piece, near, k, mate))
    for copy in passed:
        copy.wait()
    for copy in sent:
        copy.wait_send()


def layer_kernel(chans, hids, part, gain, normed_ref, own_ref, parts, gath, stat, whole, stats, s1, s2, s3, s4, s5):
    a, b, chips, chip, core, rows, far, mate = places(chans, hids)
    greet(rows + far + [mate])
    width = part.shape[2]
    size = part.shape[1]
    copies = [send(part.at[lax.rem(a + k, chans)], parts.at[k - 1], s1, k - 1, rows[k - 1]) for k in range(1, chans)]
    total = part[a].astype(jnp.float32)
    for k in range(chans - 1):
        copies[k].wait_recv()
        total = total + parts[k].astype(jnp.float32)
    gath[b] = total.astype(jnp.bfloat16)
    spread(lambda i: gath.at[i], None, chips, chip, core, far, mate, s2, s3)
    first = jnp.zeros((size, 1), jnp.float32)
    second = jnp.zeros((size, 1), jnp.float32)
    for i in range(hids):
        x = gath[i].astype(jnp.float32)
        first = first + jnp.sum(x, axis=1, keepdims=True)
        second = second + jnp.sum(x * x, axis=1, keepdims=True)
    mean = first / (width * hids)
    scale = lax.rsqrt(second / (width * hids) - mean * mean + epsilon)
    stat[...] = jnp.where(lax.broadcasted_iota(jnp.int32, stat.shape, 1) == 0, mean, scale)
    ratio = hids // chans
    moved = []
    for k in range(1, chans):
        to = lax.rem(a + k, chans)
        moved.append(send(stat, stats.at[a], s5, k - 1, rows[k - 1]))
        moved.append(send(gath.at[pl.ds(to * ratio, ratio)], whole.at[a], s4, k - 1, rows[k - 1]))
    for copy in copies:
        copy.wait_send()

    def emit(i, x_of, st):
        for r in range(ratio):
            cs = slice(r * width, (r + 1) * width)
            x = x_of(r)
            own_ref[i, :, cs] = x
            normed_ref[i, :, cs] = (
                (x.astype(jnp.float32) - st[:, 0:1]) * st[:, 1:2] * gain[:, cs]
            ).astype(jnp.bfloat16)

    emit(a, lambda r: gath[a * ratio + r], stat[...])
    for copy in moved:
        copy.wait()
    for k in range(1, chans):
        i = lax.rem(a + k, chans)
        emit(i, lambda r: whole[i, r], stats[i])


def layer_rows(partial, gain, chans, hids):
    tok, width = partial.shape
    size = tok // chans
    wide = gain.shape[0]
    vm = pl.BlockSpec(memory_space=pltpu.VMEM)
    dma = pltpu.SemaphoreType.DMA
    shape = jax.ShapeDtypeStruct((chans, size, wide), jnp.bfloat16)
    normed, own = pl.pallas_call(
        functools.partial(layer_kernel, chans, hids), out_shape=(shape, shape), in_specs=[vm, vm], out_specs=(vm, vm),
        scratch_shapes=[
            pltpu.VMEM((chans - 1, size, width), jnp.bfloat16), pltpu.VMEM((hids, size, width), jnp.bfloat16),
            pltpu.VMEM((size, HS), jnp.float32), pltpu.VMEM((chans, hids // chans, size, width), jnp.bfloat16),
            pltpu.VMEM((chans, size, HS), jnp.float32),
            dma((2, chans - 1)), dma((2, hids // 2 - 1)), dma((2, hids // 2)), dma((2, chans - 1)), dma((2, chans - 1))],
        compiler_params=pltpu.CompilerParams(collective_id=1, has_side_effects=True, vmem_limit_bytes=40 << 20),
        name="layer_rows",
    )(partial.reshape(chans, size, width), gain.reshape(1, wide))
    return normed.reshape(tok, wide), own.reshape(tok, wide)


def finish_kernel(chans, hids, heads, qkv, up, bias, qkv_out, hid_out, qkv_in, up_in, s1, s2, s3, s4):
    a, rows = lax.axis_index("chan"), [{"chan": lax.rem(lax.axis_index("chan") + k, chans)} for k in range(1, chans)]
    greet(rows)
    got_q = [send(qkv.at[:, lax.rem(a + k, chans)], qkv_in.at[k - 1], s1, k - 1, rows[k - 1]) for k in range(1, chans)]
    got_u = [send(up.at[lax.rem(a + k, chans)], up_in.at[k - 1], s2, k - 1, rows[k - 1]) for k in range(1, chans)]
    for copy in got_q:
        copy.wait_recv()
    for h in range(3 * heads):
        kind, hs = h // heads, slice(h % heads * HS, (h % heads + 1) * HS)
        x = qkv[kind, a, :, hs].astype(jnp.float32)
        for k in range(chans - 1):
            x = x + qkv_in[k, kind, :, hs].astype(jnp.float32)
        if h < 2 * heads:
            x = x * lax.rsqrt(jnp.mean(x * x, axis=-1, keepdims=True) + epsilon)
        qkv_out[h, a] = x.astype(jnp.bfloat16)
    put_q = [send(qkv_out.at[:, a], qkv_out.at[:, a], s3, k, peer) for k, peer in enumerate(rows)]
    for copy in got_u:
        copy.wait_recv()
    step = HS
    for n in range(up.shape[2] // step):
        cs = slice(n * step, (n + 1) * step)
        x = up[a, :, cs].astype(jnp.float32)
        for k in range(chans - 1):
            x = x + up_in[k, :, cs].astype(jnp.float32)
        x = x + bias[:, cs]
        hid_out[a, :, cs] = ((0.5 * x) * (1.0 + lax.erf(x * math.sqrt(0.5)))).astype(jnp.bfloat16)
    put_u = [send(hid_out.at[a], hid_out.at[a], s4, k, peer) for k, peer in enumerate(rows)]
    for copy in got_q + got_u:
        copy.wait_send()
    for copy in put_q + put_u:
        copy.wait()


def finish(qkv, up, bias, heads, chans, hids):
    tok, wide = qkv.shape[1:]
    size, units = tok // chans, up.shape[1]
    vm = pl.BlockSpec(memory_space=pltpu.VMEM)
    dma = pltpu.SemaphoreType.DMA
    q, u = pl.pallas_call(
        functools.partial(finish_kernel, chans, hids, heads),
        out_shape=(jax.ShapeDtypeStruct((3 * heads, chans, size, HS), jnp.bfloat16), jax.ShapeDtypeStruct((chans, size, units), jnp.bfloat16)),
        in_specs=[vm] * 3, out_specs=(vm, vm),
        scratch_shapes=[
            pltpu.VMEM((chans - 1, 3, size, wide), jnp.bfloat16), pltpu.VMEM((chans - 1, size, units), jnp.bfloat16)]
        + [dma((2, chans - 1))] * 4,
        compiler_params=pltpu.CompilerParams(collective_id=2, has_side_effects=True, vmem_limit_bytes=40 << 20),
        name="finish",
    )(qkv.reshape(3, chans, size, wide), up.reshape(chans, size, units), bias.reshape(1, units))
    return q.reshape(3, heads, tok, HS), u.reshape(tok, units)


def total_kernel(hids, term, own, out, pair, half, pieces, s1, s2, s3, s4):
    b = lax.axis_index("hid")
    chips, chip, core = hids // 2, b // 2, b % 2
    far = [{"hid": lax.rem(chip + k, chips) * 2 + core} for k in range(1, chips)]
    mate = {"hid": chip * 2 + (1 - core)}
    greet(far + [mate])
    across = send(term.at[1 - core], pair, s1, 0, mate)
    across.wait_recv()
    for i in range(chips):
        half[i] = (term[core, i].astype(jnp.float32) + pair[i].astype(jnp.float32)).astype(jnp.bfloat16)
    copies = [send(half.at[lax.rem(chip + k, chips)], pieces.at[k - 1], s2, k - 1, far[k - 1]) for k in range(1, chips)]
    value = half[chip].astype(jnp.float32)
    for k in range(chips - 1):
        copies[k].wait_recv()
        value = value + pieces[k].astype(jnp.float32)
    out[core, chip] = (value + own[core, chip].astype(jnp.float32)).astype(jnp.bfloat16)
    spread(lambda i: out.at[i % 2, i // 2], None, chips, chip, core, far, mate, s3, s4)
    across.wait_send()
    for copy in copies:
        copy.wait_send()


def total(term, own, hids):
    tok, wide = term.shape
    chips, size = hids // 2, tok // hids
    vm = pl.BlockSpec(memory_space=pltpu.VMEM)
    dma = pltpu.SemaphoreType.DMA
    out = pl.pallas_call(
        functools.partial(total_kernel, hids),
        out_shape=jax.ShapeDtypeStruct((2, chips, size, wide), jnp.bfloat16), in_specs=[vm] * 2, out_specs=vm,
        scratch_shapes=[
            pltpu.VMEM((chips, size, wide), jnp.bfloat16), pltpu.VMEM((chips, size, wide), jnp.bfloat16),
            pltpu.VMEM((chips - 1, size, wide), jnp.bfloat16),
            dma((2, 1)), dma((2, chips - 1)), dma((2, chips - 1)), dma((2, chips))],
        compiler_params=pltpu.CompilerParams(collective_id=3, has_side_effects=True, vmem_limit_bytes=40 << 20),
        name="total",
    )(term.reshape(2, chips, size, wide), own.reshape(2, chips, size, wide))
    return out.reshape(tok, wide)


def on_device(
    chans,
    hids,
    pixels,
    patch_weight,
    channel_embed,
    pool_query,
    group_mix,
    assign,
    ln_gain,
    w_qkv,
    w_up,
    b_up,
    w_out,
    w_down,
):
    tok_count = pixels.shape[1]
    width_hid = patch_weight.shape[2]
    heads_dev = width_hid // HS
    partial_value = pool(pixels.shape[1], pixels, patch_weight, channel_embed, pool_query, group_mix, assign)
    normed_input, own_cols = layer_rows(partial_value, ln_gain, chans, hids)
    qkv_part = jnp.einsum("td,dke->kte", normed_input, w_qkv, preferred_element_type=jnp.float32)
    up_part = jnp.dot(normed_input, w_up, preferred_element_type=jnp.float32)
    qkv_rows, hidden = finish(
        qkv_part.astype(jnp.bfloat16), up_part.astype(jnp.bfloat16), b_up, heads_dev, chans, hids
    )
    images = tok_count // PATCHES
    queries, keys, values = qkv_rows.reshape(3, heads_dev, images, PATCHES, HS)
    scores = jnp.einsum("hbqe,hbke->hbqk", queries, keys, preferred_element_type=jnp.float32) * (
        2.0 / math.sqrt(HS)
    )
    expo = jnp.exp(scores)
    probs = (expo / jnp.sum(expo, axis=-1, keepdims=True)).astype(jnp.bfloat16)
    attended = jnp.einsum("hbqk,hbke->bqhe", probs, values, preferred_element_type=jnp.float32)
    attended = attended.astype(jnp.bfloat16).reshape(tok_count, width_hid)
    term = jnp.dot(attended, w_out, preferred_element_type=jnp.float32) + jnp.dot(
        hidden, w_down, preferred_element_type=jnp.float32
    )
    term = term.astype(jnp.bfloat16)
    if tok_count % (16 * hids) == 0:
        return total(term, own_cols, hids)
    mixed = lax.psum(term, "hid").astype(jnp.float32)
    return (own_cols.astype(jnp.float32) + mixed).astype(jnp.bfloat16)


def solution(mesh):
    in_specs = (
        P("chan", None, None),
        P("chan", None, "hid"),
        P("chan", "hid"),
        P("chan", "hid"),
        P("chan", "hid"),
        P("chan"),
        P("chan"),
        P("chan", None, "hid"),
        P("chan", "hid"),
        P("hid"),
        P("hid", "chan"),
        P("hid", "chan"),
    )
    out_specs = P(None, "chan")
    chans, hids = mesh.shape["chan"], mesh.shape["hid"]
    return jax.shard_map(
        functools.partial(on_device, chans, hids), mesh=mesh, in_specs=in_specs, out_specs=out_specs, check_vma=False
    )
```

```python
import functools
import math

import jax
import jax.numpy as jnp
from jax import lax
from jax.experimental import pallas as pl
from jax.experimental.pallas import tpu as pltpu
from jax.sharding import PartitionSpec as P

HS = 128
PATCHES = 256


epsilon = 1e-06


ACROSS = (((1,), (1,)), ((), ()))
LOG2E = math.log2(math.e)
SLOT = 16
ROWS = 256
CPS = 4


def pool_setup(groups, size, query, mix, emb, quer, pick, shift, mixs, embs, fan):
    width = quer.shape[1]
    own = lax.broadcasted_iota(jnp.int32, (SLOT, width), 0) == lax.broadcasted_iota(jnp.int32, (SLOT, width), 1) // HS
    q = query[...].astype(jnp.float32)
    m = mix[...].astype(jnp.float32) * math.sqrt(0.5)
    pick[...] = jnp.where(own, 1.0, 0.0).astype(jnp.bfloat16)
    for g in range(groups):
        row = jnp.where(own, q[g:g+1, :], 0.0)
        rs = slice(g*SLOT, (g+1)*SLOT)
        quer[rs, :] = row.astype(jnp.bfloat16)
        n = jnp.sqrt(jnp.sum(row * row, axis=1, keepdims=True)) * LOG2E
        shift[rs, :] = jnp.broadcast_to(n, (SLOT, HS))
        mixs[g] = m[g:g+1]
    for c in range(0, emb.shape[0], 8):
        e = emb[c:c+8, :].astype(jnp.float32) * math.sqrt(0.5)
        for k in range(8):
            embs[c+k] = e[k:k+1]
    kind = lax.rem(lax.broadcasted_iota(jnp.int32, (HS, width), 0), HS // 2)
    head = lax.broadcasted_iota(jnp.int32, (HS, width), 1) // HS
    for j in range(size):
        fan[j] = jnp.where(kind == j * 8 + head, 1.0, 0.0).astype(jnp.bfloat16)

def features(tok, px_of, pw_of, bias, put):
    width = bias.shape[1]
    step = min(256, width)
    R = min(ROWS, tok)
    for n in range(width // step):
        cs = slice(n*step, (n+1)*step)
        for r in range(0, tok, R):
            e = jnp.dot(px_of(r, R), pw_of(cs), preferred_element_type=jnp.float32)
            u = e * math.sqrt(0.5) + bias[:, cs]
            g = (u * (1.0 + lax.erf(u))).astype(jnp.bfloat16)
            put(r, R, cs, g, g * g)

def weigh(tok, g, s, local, quer, pick, shift):
    rs = pl.ds(pl.multiple_of(local * SLOT, SLOT), SLOT)
    dots = lax.dot_general(quer[rs, :], g[...], ACROSS, preferred_element_type=jnp.float32)
    total = lax.dot_general(pick[...], s[...], ACROSS, preferred_element_type=jnp.float32)
    sh = jnp.concatenate([shift[rs, :]] * (tok // HS), axis=1)
    score = dots * lax.rsqrt(total * (1.0 / HS) + 2 * epsilon) * (LOG2E / math.sqrt(HS))
    return jnp.exp2(score - sh)[0:8, :]

def merge(groups, size, tok, order, feat, wts, mixs, fan, acc):
    width = feat.shape[2]
    step = min(256, width)
    def group(g, _):
        cs = [order[g*size + j] for j in range(size)]
        for b in range(0, tok, HS):
            bs = slice(b, b + HS)
            ws = [wts[c, :, bs] for c in cs]
            den = ws[0]
            for w in ws[1:]:
                den = den + w
            inv = 1.0 / den
            w = jnp.concatenate([w * inv for w in ws], axis=0)
            hi = w.astype(jnp.bfloat16).astype(jnp.float32)
            both = jnp.transpose(jnp.concatenate([hi, w - hi], axis=0))
            lhs = both.astype(jnp.bfloat16)
            for n in range(width // step):
                ns = slice(n*step, (n+1)*step)
                p = None
                for j in range(size):
                    t = jnp.dot(lhs, fan[j, :, ns], preferred_element_type=jnp.float32) * feat[cs[j], bs, ns].astype(jnp.float32)
                    p = t if p is None else p + t
                acc[bs, ns] += p * mixs[g, :, ns]
        return 0
    lax.fori_loop(0, groups, group, 0)

def pool_kernel(groups, size, order, assign, pix, pw, emb, query, mix, out, feat, wts, acc, quer, pick, shift, mixs, embs, fan, g0, g1, s0, s1):
    t = pl.program_id(0); c = pl.program_id(1)
    tok = out.shape[0]
    gb, sb = (g0, g1), (s0, s1)
    @pl.when((t == 0) & (c == 0))
    def _():
        pool_setup(groups, size, query, mix, emb, quer, pick, shift, mixs, embs, fan)
    @pl.when(c == 0)
    def _():
        acc[...] = jnp.zeros_like(acc)
    def back(k):
        cc = c * CPS + k
        wts[cc] = weigh(tok, gb[k % 2], sb[k % 2], lax.rem(assign[cc], groups), quer, pick, shift)
    for k in range(CPS):
        cc = c * CPS + k
        def put(r, R, cs, g, s):
            feat[cc, r:r+R, cs] = g
            gb[k % 2][r:r+R, cs] = g
            sb[k % 2][r:r+R, cs] = s
        features(tok, lambda r, R: pix[k, r:r+R, :], lambda cs: pw[k, :, cs], embs[cc], put)
        if k: back(k - 1)
    back(CPS - 1)
    @pl.when(c == pl.num_programs(1)-1)
    def _():
        merge(groups, size, tok, order, feat, wts, mixs, fan, acc)
        out[...] = acc[...].astype(jnp.bfloat16)

def pool(T, pixels, patch_weight, channel_embed, pool_query, group_mix, assign):
    chans, tok, p2 = pixels.shape
    width = patch_weight.shape[2]
    groups = pool_query.shape[0]
    size = chans // groups
    idx = jnp.arange(chans, dtype=jnp.int32)
    key = assign * chans + idx
    rank = jnp.sum((key[None, :] < key[:, None]).astype(jnp.int32), axis=1)
    order = jnp.sum(jnp.where(rank[None, :] == idx[:, None], idx[None, :], 0), axis=1).astype(jnp.int32)
    full = lambda s: pl.BlockSpec(s, lambda t, c, *_: (0,)*len(s))
    vm = pltpu.VMEM
    spec = pltpu.PrefetchScalarGridSpec(num_scalar_prefetch=2, grid=(tok//T, chans//CPS),
        in_specs=[pl.BlockSpec((CPS,T,p2), lambda t,c,*_:(c,t,0)), pl.BlockSpec((CPS,p2,width), lambda t,c,*_:(c,0,0)),
          full((chans,width)), full((groups,width)), full((groups,width))],
        out_specs=pl.BlockSpec((T,width), lambda t,c,*_:(t,0)),
        scratch_shapes=[vm((chans,T,width), jnp.bfloat16), vm((chans,8,T), jnp.float32),
          vm((T,width), jnp.float32), vm((groups*SLOT,width), jnp.bfloat16), vm((SLOT,width), jnp.bfloat16),
          vm((groups*SLOT,HS), jnp.float32), vm((groups,1,width), jnp.float32), vm((chans,1,width), jnp.float32),
          vm((size,HS,width), jnp.bfloat16)] + [vm((T,width), jnp.bfloat16)]*4)
    return pl.pallas_call(functools.partial(pool_kernel, groups, size), grid_spec=spec, out_shape=jax.ShapeDtypeStruct((tok,width), jnp.bfloat16),
        compiler_params=pltpu.CompilerParams(dimension_semantics=("arbitrary","arbitrary"), vmem_limit_bytes=62<<20), name="pool")(
        order, assign, pixels, patch_weight, channel_embed, pool_query, group_mix)
def head_norm(values):
    return values * lax.rsqrt(jnp.mean(values * values, axis=-1, keepdims=True) + epsilon)


MESH = pl.DeviceIdType.MESH


def greet(peers):
    gate = pltpu.get_barrier_semaphore()
    for peer in peers:
        pl.semaphore_signal(gate, inc=1, device_id=peer, device_id_type=MESH)
    pl.semaphore_wait(gate, len(peers))


def send(src, dst, sems, slot, peer):
    copy = pltpu.make_async_remote_copy(
        src_ref=src, dst_ref=dst, send_sem=sems.at[0, slot], recv_sem=sems.at[1, slot],
        device_id=peer, device_id_type=MESH)
    copy.start()
    return copy


def places(chans, hids):
    a, b = lax.axis_index("chan"), lax.axis_index("hid")
    chips, chip, core = hids // 2, b // 2, b % 2
    rows = [{"chan": lax.rem(a + k, chans)} for k in range(1, chans)]
    far = [{"hid": lax.rem(chip + k, chips) * 2 + core} for k in range(1, chips)]
    return a, b, chips, chip, core, rows, far, {"hid": chip * 2 + (1 - core)}


def spread(src_of, slots, chips, chip, core, far, mate, away, near):
    sent = [send(src_of(chip * 2 + core), src_of(chip * 2 + core), away, k, peer) for k, peer in enumerate(far)]
    mine = src_of(chip * 2 + core)
    passed = [send(mine, mine, near, 0, mate)]
    for k in range(1, chips):
        sent[k - 1].wait_recv()
        piece = src_of(lax.rem(chip + chips - k, chips) * 2 + core)
        passed.append(send(piece, piece, near, k, mate))
    for copy in passed:
        copy.wait()
    for copy in sent:
        copy.wait_send()


def layer_kernel(chans, hids, part, gain, normed_ref, own_ref, parts, gath, stat, whole, stats, s1, s2, s3, s4, s5):
    a, b, chips, chip, core, rows, far, mate = places(chans, hids)
    greet(rows + far + [mate])
    width = part.shape[2]
    size = part.shape[1]
    copies = [send(part.at[lax.rem(a + k, chans)], parts.at[k - 1], s1, k - 1, rows[k - 1]) for k in range(1, chans)]
    total = part[a].astype(jnp.float32)
    for k in range(chans - 1):
        copies[k].wait_recv()
        total = total + parts[k].astype(jnp.float32)
    gath[b] = total.astype(jnp.bfloat16)
    spread(lambda i: gath.at[i], None, chips, chip, core, far, mate, s2, s3)
    first = jnp.zeros((size, 1), jnp.float32)
    second = jnp.zeros((size, 1), jnp.float32)
    for i in range(hids):
        x = gath[i].astype(jnp.float32)
        first = first + jnp.sum(x, axis=1, keepdims=True)
        second = second + jnp.sum(x * x, axis=1, keepdims=True)
    mean = first / (width * hids)
    scale = lax.rsqrt(second / (width * hids) - mean * mean + epsilon)
    stat[...] = jnp.where(lax.broadcasted_iota(jnp.int32, stat.shape, 1) == 0, mean, scale)
    ratio = hids // chans
    moved = []
    for k in range(1, chans):
        to = lax.rem(a + k, chans)
        moved.append(send(stat, stats.at[a], s5, k - 1, rows[k - 1]))
        moved.append(send(gath.at[pl.ds(to * ratio, ratio)], whole.at[a], s4, k - 1, rows[k - 1]))
    for copy in copies:
        copy.wait_send()

    def emit(i, x_of, st):
        for r in range(ratio):
            cs = slice(r * width, (r + 1) * width)
            x = x_of(r)
            own_ref[i, :, cs] = x
            normed_ref[i, :, cs] = (
                (x.astype(jnp.float32) - st[:, 0:1]) * st[:, 1:2] * gain[:, cs]
            ).astype(jnp.bfloat16)

    emit(a, lambda r: gath[a * ratio + r], stat[...])
    for copy in moved:
        copy.wait()
    for k in range(1, chans):
        i = lax.rem(a + k, chans)
        emit(i, lambda r: whole[i, r], stats[i])


def layer_rows(partial, gain, chans, hids):
    tok, width = partial.shape
    size = tok // chans
    wide = gain.shape[0]
    vm = pl.BlockSpec(memory_space=pltpu.VMEM)
    dma = pltpu.SemaphoreType.DMA
    shape = jax.ShapeDtypeStruct((chans, size, wide), jnp.bfloat16)
    normed, own = pl.pallas_call(
        functools.partial(layer_kernel, chans, hids), out_shape=(shape, shape), in_specs=[vm, vm], out_specs=(vm, vm),
        scratch_shapes=[
            pltpu.VMEM((chans - 1, size, width), jnp.bfloat16), pltpu.VMEM((hids, size, width), jnp.bfloat16),
            pltpu.VMEM((size, HS), jnp.float32), pltpu.VMEM((chans, hids // chans, size, width), jnp.bfloat16),
            pltpu.VMEM((chans, size, HS), jnp.float32),
            dma((2, chans - 1)), dma((2, hids // 2 - 1)), dma((2, hids // 2)), dma((2, chans - 1)), dma((2, chans - 1))],
        compiler_params=pltpu.CompilerParams(collective_id=1, has_side_effects=True, vmem_limit_bytes=40 << 20),
        name="layer_rows",
    )(partial.reshape(chans, size, width), gain.reshape(1, wide))
    return normed.reshape(tok, wide), own.reshape(tok, wide)


def finish_kernel(chans, hids, heads, qkv, up, bias, qkv_out, hid_out, qkv_in, up_in, s1, s2, s3, s4):
    a, rows = lax.axis_index("chan"), [{"chan": lax.rem(lax.axis_index("chan") + k, chans)} for k in range(1, chans)]
    greet(rows)
    got_q = [send(qkv.at[:, lax.rem(a + k, chans)], qkv_in.at[k - 1], s1, k - 1, rows[k - 1]) for k in range(1, chans)]
    got_u = [send(up.at[lax.rem(a + k, chans)], up_in.at[k - 1], s2, k - 1, rows[k - 1]) for k in range(1, chans)]
    for copy in got_q:
        copy.wait_recv()
    for h in range(3 * heads):
        kind, hs = h // heads, slice(h % heads * HS, (h % heads + 1) * HS)
        x = qkv[kind, a, :, hs].astype(jnp.float32)
        for k in range(chans - 1):
            x = x + qkv_in[k, kind, :, hs].astype(jnp.float32)
        if h < 2 * heads:
            x = x * lax.rsqrt(jnp.mean(x * x, axis=-1, keepdims=True) + epsilon)
        qkv_out[h, a] = x.astype(jnp.bfloat16)
    put_q = [send(qkv_out.at[:, a], qkv_out.at[:, a], s3, k, peer) for k, peer in enumerate(rows)]
    for copy in got_u:
        copy.wait_recv()
    step = HS
    for n in range(up.shape[2] // step):
        cs = slice(n * step, (n + 1) * step)
        x = up[a, :, cs].astype(jnp.float32)
        for k in range(chans - 1):
            x = x + up_in[k, :, cs].astype(jnp.float32)
        x = x + bias[:, cs]
        hid_out[a, :, cs] = ((0.5 * x) * (1.0 + lax.erf(x * math.sqrt(0.5)))).astype(jnp.bfloat16)
    put_u = [send(hid_out.at[a], hid_out.at[a], s4, k, peer) for k, peer in enumerate(rows)]
    for copy in got_q + got_u:
        copy.wait_send()
    for copy in put_q + put_u:
        copy.wait()


def finish(qkv, up, bias, heads, chans, hids):
    tok, wide = qkv.shape[1:]
    size, units = tok // chans, up.shape[1]
    vm = pl.BlockSpec(memory_space=pltpu.VMEM)
    dma = pltpu.SemaphoreType.DMA
    q, u = pl.pallas_call(
        functools.partial(finish_kernel, chans, hids, heads),
        out_shape=(jax.ShapeDtypeStruct((3 * heads, chans, size, HS), jnp.bfloat16), jax.ShapeDtypeStruct((chans, size, units), jnp.bfloat16)),
        in_specs=[vm] * 3, out_specs=(vm, vm),
        scratch_shapes=[
            pltpu.VMEM((chans - 1, 3, size, wide), jnp.bfloat16), pltpu.VMEM((chans - 1, size, units), jnp.bfloat16)]
        + [dma((2, chans - 1))] * 4,
        compiler_params=pltpu.CompilerParams(collective_id=2, has_side_effects=True, vmem_limit_bytes=40 << 20),
        name="finish",
    )(qkv.reshape(3, chans, size, wide), up.reshape(chans, size, units), bias.reshape(1, units))
    return q.reshape(3, heads, tok, HS), u.reshape(tok, units)


def total_kernel(hids, term, own, out, pair, half, pieces, s1, s2, s3, s4):
    b = lax.axis_index("hid")
    chips, chip, core = hids // 2, b // 2, b % 2
    far = [{"hid": lax.rem(chip + k, chips) * 2 + core} for k in range(1, chips)]
    mate = {"hid": chip * 2 + (1 - core)}
    greet(far + [mate])
    across = send(term.at[1 - core], pair, s1, 0, mate)
    across.wait_recv()
    for i in range(chips):
        half[i] = (term[core, i].astype(jnp.float32) + pair[i].astype(jnp.float32)).astype(jnp.bfloat16)
    copies = [send(half.at[lax.rem(chip + k, chips)], pieces.at[k - 1], s2, k - 1, far[k - 1]) for k in range(1, chips)]
    value = half[chip].astype(jnp.float32)
    for k in range(chips - 1):
        copies[k].wait_recv()
        value = value + pieces[k].astype(jnp.float32)
    out[core, chip] = (value + own[core, chip].astype(jnp.float32)).astype(jnp.bfloat16)
    spread(lambda i: out.at[i % 2, i // 2], None, chips, chip, core, far, mate, s3, s4)
    across.wait_send()
    for copy in copies:
        copy.wait_send()


def total(term, own, hids):
    tok, wide = term.shape
    chips, size = hids // 2, tok // hids
    vm = pl.BlockSpec(memory_space=pltpu.VMEM)
    dma = pltpu.SemaphoreType.DMA
    out = pl.pallas_call(
        functools.partial(total_kernel, hids),
        out_shape=jax.ShapeDtypeStruct((2, chips, size, wide), jnp.bfloat16), in_specs=[vm] * 2, out_specs=vm,
        scratch_shapes=[
            pltpu.VMEM((chips, size, wide), jnp.bfloat16), pltpu.VMEM((chips, size, wide), jnp.bfloat16),
            pltpu.VMEM((chips - 1, size, wide), jnp.bfloat16),
            dma((2, 1)), dma((2, chips - 1)), dma((2, chips - 1)), dma((2, chips))],
        compiler_params=pltpu.CompilerParams(collective_id=3, has_side_effects=True, vmem_limit_bytes=40 << 20),
        name="total",
    )(term.reshape(2, chips, size, wide), own.reshape(2, chips, size, wide))
    return out.reshape(tok, wide)


def column_steps(width, most=384):
    step = max(s for s in range(HS, most + 1, HS) if width % s == 0)
    return [slice(n, n + step) for n in range(0, width, step)]


class Tail:
    def __init__(self, chans, hids, refs):
        self.__dict__.update(refs)
        self.chans, self.hids = chans, hids
        self.a, self.b, self.chips, self.chip, self.core, self.rows, self.far, self.mate = places(chans, hids)
        self.y, self.x = self.a // 2, self.a % 2
        self.across_x, self.across_y = {"chan": self.y * 2 + 1 - self.x}, {"chan": (1 - self.y) * 2 + self.x}
        self.used, self.open = 0, []

    def put(self, src, dst, peer):
        slot = self.used
        self.used += 1
        copy = pltpu.make_async_remote_copy(
            src_ref=src, dst_ref=dst, send_sem=self.sems.at[0, slot], recv_sem=self.sems.at[1, slot],
            device_id=peer, device_id_type=MESH)
        copy.start()
        self.open.append(copy)
        return copy

    def drain(self):
        for copy in self.open:
            copy.wait_send()

    def scatter(self, t):
        a, chans = self.a, self.chans
        self.s_copies = getattr(self, "s_copies", {})
        self.s_copies[t] = [
            self.put(self.part.at[t, lax.rem(a + k, chans)], self.parts.at[t, k - 1], self.rows[k - 1]) for k in range(1, chans)]

    def collect(self, t):
        total = self.part[t, self.a].astype(jnp.float32)
        for k, copy in enumerate(self.s_copies[t]):
            copy.wait_recv()
            total = total + self.parts[t, k].astype(jnp.float32)
        b = self.b
        self.gath[t, b] = total.astype(jnp.bfloat16)
        mine = self.gath.at[t, b]
        self.g_far = getattr(self, "g_far", {})
        self.g_near = getattr(self, "g_near", {})
        self.g_far[t] = [self.put(mine, mine, peer) for peer in self.far]
        self.g_near[t] = [self.put(mine, mine, self.mate)]

    def relay(self, t):
        for k in range(1, self.chips):
            self.g_far[t][k - 1].wait_recv()
            piece = self.gath.at[t, lax.rem(self.chip + self.chips - k, self.chips) * 2 + self.core]
            self.g_near[t].append(self.put(piece, piece, self.mate))

    def exchange(self, t):
        for copy in self.g_near[t]:
            copy.wait_recv()
        size, width = self.gath.shape[2:]
        first = jnp.zeros((size, 1), jnp.float32)
        second = jnp.zeros((size, 1), jnp.float32)
        for i in range(self.hids):
            x = self.gath[t, i].astype(jnp.float32)
            first = first + jnp.sum(x, axis=1, keepdims=True)
            second = second + jnp.sum(x * x, axis=1, keepdims=True)
        mean = first / (width * self.hids)
        scale = lax.rsqrt(second / (width * self.hids) - mean * mean + epsilon)
        self.stat[t] = jnp.where(lax.broadcasted_iota(jnp.int32, (size, HS), 1) == 0, mean, scale)
        self.c_stat = getattr(self, "c_stat", {})
        self.c_piece = getattr(self, "c_piece", {})
        a, chans = self.a, self.chans
        self.c_stat[t] = [self.put(self.stat.at[t], self.stats.at[t, a], peer) for peer in self.rows]
        self.c_piece[t] = [
            self.put(self.gath.at[t, lax.rem(a + k, chans) * 2 + self.core], self.whole.at[t, a, self.core], self.rows[k - 1])
            for k in range(1, chans)]

    def share(self, t):
        self.c_near = getattr(self, "c_near", {})
        self.c_near[t] = []
        for k in range(1, self.chans):
            self.c_piece[t][k - 1].wait_recv()
            piece = self.whole.at[t, lax.rem(self.a + self.chans - k, self.chans), self.core]
            self.c_near[t].append(self.put(piece, piece, self.mate))

    def norm(self, t):
        size, width = self.gath.shape[2:]

        def emit(i, x_of, st):
            for r in range(2):
                cs = slice(r * width, (r + 1) * width)
                x = x_of(r)
                self.own[t, i, :, cs] = x
                self.normed[t, i, :, cs] = (
                    (x.astype(jnp.float32) - st[:, 0:1]) * st[:, 1:2] * self.gain[:, cs]).astype(jnp.bfloat16)

        emit(self.a, lambda r: self.gath[t, self.a * 2 + r], self.stat[t])
        for copy in self.c_stat[t] + self.c_near[t]:
            copy.wait_recv()
        for k in range(1, self.chans):
            i = lax.rem(self.a + k, self.chans)
            emit(i, lambda r: self.whole[t, i, r], self.stats[t, i])

    def multiply(self, t, kind):
        buf, weights = self.units[kind][0], self.units[kind][4]
        size = buf.shape[3]
        wide = buf.shape[4]
        step = min(256, self.w_qkv.shape[2])
        x = self.normed[t].reshape(4 * size, self.normed.shape[3])
        per = weights.shape[-1]

        for k in range(wide // per):
            def tile(n, _):
                off = pl.multiple_of(n * step, step)
                w = weights[k, :, pl.ds(off, step)] if kind == "qkv" else weights[:, pl.ds(off, step)]
                e = jnp.dot(x, w, preferred_element_type=jnp.float32).astype(jnp.bfloat16)
                buf[t, :, :, :, pl.ds(pl.multiple_of(k * per + off, step), step)] = e.reshape(2, 2, size, step)
                return 0
            lax.fori_loop(0, per // step, tile, 0)

    def halves(self, kind):
        wide = self.units[kind][0].shape[4]
        return slice(0, wide // 2), slice(wide // 2, wide)

    def reduce1(self, t, kind):
        buf, got1 = self.units[kind][:2]
        left, right = self.halves(kind)
        self.d1 = getattr(self, "d1", {})
        self.d1[t, kind] = (
            self.put(buf.at[t, :, 1 - self.x, :, left], got1.at[t, 0], self.across_x),
            self.put(buf.at[t, 1 - self.y, :, :, right], got1.at[t, 1], self.across_y))

    def reduce2(self, t, kind):
        buf, got1, mid, got2 = self.units[kind][:4]
        left, right = self.halves(kind)
        self.d2 = getattr(self, "d2", {})
        for copy in self.d1[t, kind]:
            copy.wait_recv()
        for side in range(2):
            base = (left, right)[side].start
            for cs in column_steps(got1.shape[4]):
                here = slice(base + cs.start, base + cs.stop)
                mine = buf[t, 1 - self.y, self.x, :, here] if side == 0 else buf[t, self.y, 1 - self.x, :, here]
                got = got1[t, 0, 1 - self.y, :, cs] if side == 0 else got1[t, 1, 1 - self.x, :, cs]
                mid[t, side, :, cs] = (mine.astype(jnp.float32) + got.astype(jnp.float32)).astype(jnp.bfloat16)
            self.d2[t, kind, side] = self.put(mid.at[t, side], got2.at[t, side], (self.across_y, self.across_x)[side])

    def act(self, t, kind):
        buf, got1, _, got2, _, full = self.units[kind]
        left, right = self.halves(kind)
        self.e1 = getattr(self, "e1", {})
        rotated = 2 * self.w_qkv.shape[2]
        for side in range(2):
            self.d2[t, kind, side].wait_recv()
            base = (left, right)[side].start
            for c in range(0, got1.shape[4], HS):
                cs = slice(c, c + HS)
                here = slice(base + c, base + c + HS)
                v = buf[t, self.y, self.x, :, here].astype(jnp.float32) + got2[t, side, :, cs].astype(jnp.float32)
                v = v + (got1[t, 0, self.y, :, cs] if side == 0 else got1[t, 1, self.x, :, cs]).astype(jnp.float32)
                if kind == "up":
                    v = v + self.bias[:, here]
                    v = (0.5 * v) * (1.0 + lax.erf(v * math.sqrt(0.5)))
                elif base + c < rotated:
                    v = v * lax.rsqrt(jnp.mean(v * v, axis=-1, keepdims=True) + epsilon)
                full[t, self.y, self.x, :, here] = v.astype(jnp.bfloat16)
            mine = full.at[t, self.y, self.x, :, (left, right)[side]]
            self.e1[t, kind, side] = self.put(mine, mine, (self.across_y, self.across_x)[side])

    def gather2(self, t, kind):
        full = self.units[kind][5]
        left, right = self.halves(kind)
        self.e2 = getattr(self, "e2", {})
        for side in range(2):
            self.e1[t, kind, side].wait_recv()
            mine = full.at[t, :, self.x, :, left] if side == 0 else full.at[t, self.y, :, :, right]
            self.e2[t, kind, side] = self.put(mine, mine, (self.across_x, self.across_y)[side])

    def whole_unit(self, t, kind):
        for side in range(2):
            self.e2[t, kind, side].wait_recv()

    def attend(self, chunks):
        full = self.units["qkv"][5]
        size = full.shape[3]
        wide = self.w_qkv.shape[2]
        tok = chunks * 4 * size

        def head(h, _):
            def take(kind):
                cs = pl.ds(pl.multiple_of(kind * wide + h * HS, HS), HS)
                return full[:, :, :, :, cs].reshape(tok, HS)
            q, k, v = take(0), take(1), take(2)
            for r in range(0, tok, PATCHES):
                rs = slice(r, r + PATCHES)
                scores = lax.dot_general(q[rs], k[rs], ACROSS, preferred_element_type=jnp.float32) * (2.0 / math.sqrt(HS))
                expo = jnp.exp(scores)
                probs = (expo * (1.0 / jnp.sum(expo, axis=-1, keepdims=True))).astype(jnp.bfloat16)
                got = jnp.dot(probs, v[rs], preferred_element_type=jnp.float32).astype(jnp.bfloat16)
                self.attended[rs, pl.ds(pl.multiple_of(h * HS, HS), HS)] = got
            return 0

        lax.fori_loop(0, wide // HS, head, 0)

    def down(self, t):
        full = self.units["up"][5]
        size = full.shape[3]
        rows = 4 * size
        wide = self.w_out.shape[1]
        step = min(256, wide)
        hidden = full[t].reshape(rows, full.shape[4])
        att = self.attended[t * rows:(t + 1) * rows]

        def tile(n, _):
            cs = pl.ds(pl.multiple_of(n * step, step), step)
            e = jnp.dot(hidden, self.w_down[:, cs], preferred_element_type=jnp.float32)
            e = e + jnp.dot(att, self.w_out[:, cs], preferred_element_type=jnp.float32)
            self.term[t, :, :, :, cs] = e.astype(jnp.bfloat16).reshape(2, self.chips, rows // self.hids, step)
            return 0

        lax.fori_loop(0, wide // step, tile, 0)
        self.f1 = getattr(self, "f1", {})
        self.f1[t] = self.put(self.term.at[t, 1 - self.core], self.pair.at[t], self.mate)

    def total1(self, t):
        self.f1[t].wait_recv()
        self.f2 = getattr(self, "f2", {})
        chips, chip = self.chips, self.chip
        for i in range(chips):
            self.half[t, i] = (
                self.term[t, self.core, i].astype(jnp.float32) + self.pair[t, i].astype(jnp.float32)).astype(jnp.bfloat16)
        self.f2[t] = [
            self.put(self.half.at[t, lax.rem(chip + k, chips)], self.pieces.at[t, k - 1], self.far[k - 1]) for k in range(1, chips)]

    def total2(self, t):
        value = self.half[t, self.chip].astype(jnp.float32)
        for k, copy in enumerate(self.f2[t]):
            copy.wait_recv()
            value = value + self.pieces[t, k].astype(jnp.float32)
        core, chip, chips = self.core, self.chip, self.chips
        own = self.own_rows(t)
        self.out[t, core, chip] = (value + own).astype(jnp.bfloat16)
        mine = self.out.at[t, core, chip]
        self.f3 = getattr(self, "f3", {})
        self.f4 = getattr(self, "f4", {})
        self.f3[t] = [self.put(mine, mine, peer) for peer in self.far]
        self.f4[t] = [self.put(mine, mine, self.mate)]

    def own_rows(self, t):
        rows = self.out.shape[3]
        place = (self.core * self.chips + self.chip) * rows
        size = self.own.shape[2]
        return self.own[t, place // size, pl.ds(pl.multiple_of(lax.rem(place, size), rows), rows), :].astype(jnp.float32)

    def total3(self, t):
        for k in range(1, self.chips):
            self.f3[t][k - 1].wait_recv()
            piece = self.out.at[t, self.core, lax.rem(self.chip + self.chips - k, self.chips)]
            self.f4[t].append(self.put(piece, piece, self.mate))

    def total4(self, t):
        for copy in self.f4[t]:
            copy.wait_recv()


def tail_kernel(chans, hids, chunks, *refs):
    names = ["part", "gain", "bias", "wq_hbm", "wu_hbm", "wo_hbm", "wd_hbm", "out", "parts", "gath", "stat", "stats", "whole",
             "own", "normed", "q0", "q1", "q2", "q3", "q4", "u0", "u1", "u2", "u3", "u4", "attended", "term", "pair", "half",
             "pieces", "w_qkv", "w_up", "w_out", "w_down", "sems", "loads"]
    refs = dict(zip(names, refs))
    refs["units"] = {
        "qkv": [refs["q0"], refs["q1"], refs["q2"], refs["q3"], refs["w_qkv"], refs["q4"]],
        "up": [refs["u0"], refs["u1"], refs["u2"], refs["u3"], refs["w_up"], refs["u4"]]}
    s = Tail(chans, hids, refs)
    loads = []
    for i, (src, dst) in enumerate([("wq_hbm", "w_qkv"), ("wu_hbm", "w_up"), ("wo_hbm", "w_out"), ("wd_hbm", "w_down")]):
        loads.append(pltpu.make_async_copy(refs[src], refs[dst], refs["loads"].at[i]))
        loads[-1].start()
    greet(s.rows + s.far + [s.mate])
    every = range(chunks)
    for step in (s.scatter, s.collect, s.relay, s.exchange):
        for t in every:
            step(t)
    todo = []
    for t in every:
        s.share(t)
        s.norm(t)
        if t == 0:
            loads[0].wait()
        s.multiply(t, "qkv")
        s.reduce1(t, "qkv")
        if t == 0:
            loads[1].wait()
        if t:
            s.reduce2(t - 1, "qkv")
        s.multiply(t, "up")
        s.reduce1(t, "up")
        if t:
            s.reduce2(t - 1, "up")
            s.act(t - 1, "qkv")
            s.act(t - 1, "up")
            s.gather2(t - 1, "qkv")
    last = chunks - 1
    s.reduce2(last, "qkv")
    s.reduce2(last, "up")
    if last:
        s.gather2(last - 1, "up")
    s.act(last, "qkv")
    s.act(last, "up")
    s.gather2(last, "qkv")
    s.gather2(last, "up")
    for t in every:
        s.whole_unit(t, "qkv")
    s.attend(chunks)
    loads[2].wait()
    loads[3].wait()
    for t in every:
        s.whole_unit(t, "up")
        s.down(t)
        if t:
            s.total1(t - 1)
            s.total2(t - 1)
    s.total1(last)
    if last:
        s.total3(last - 1)
    s.total2(last)
    s.total3(last)
    for t in every:
        s.total4(t)
    s.drain()


def tail(partial, gain, bias, w_qkv, w_up, w_out, w_down, chans, hids, chunks):
    tok, width = partial.shape
    rows = tok // chunks
    size = rows // chans
    wide = gain.shape[0]
    chips = hids // 2
    qw, units = w_qkv.shape[0] * w_qkv.shape[2], w_up.shape[1]
    bf, vm, hbm = jnp.bfloat16, pl.BlockSpec(memory_space=pltpu.VMEM), pl.BlockSpec(memory_space=pl.ANY)
    V = pltpu.VMEM

    def unit(w):
        return [V((chunks, 2, 2, size, w), bf), V((chunks, 2, 2, size, w // 2), bf), V((chunks, 2, size, w // 2), bf),
                V((chunks, 2, size, w // 2), bf), V((chunks, 2, 2, size, w), bf)]

    few = rows // hids
    out = pl.pallas_call(
        functools.partial(tail_kernel, chans, hids, chunks),
        out_shape=jax.ShapeDtypeStruct((chunks, 2, chips, few, wide), bf),
        in_specs=[vm] * 3 + [hbm] * 4, out_specs=vm,
        scratch_shapes=[
            V((chunks, chans - 1, size, width), bf), V((chunks, hids, size, width), bf), V((chunks, size, HS), jnp.float32),
            V((chunks, chans, size, HS), jnp.float32), V((chunks, chans, 2, size, width), bf),
            V((chunks, chans, size, wide), bf), V((chunks, chans, size, wide), bf)]
        + unit(qw) + unit(units)
        + [V((tok, w_out.shape[0]), bf), V((chunks, 2, chips, few, wide), bf), V((chunks, chips, few, wide), bf),
           V((chunks, chips, few, wide), bf), V((chunks, chips - 1, few, wide), bf),
           V(w_qkv.shape, bf), V(w_up.shape, bf), V(w_out.shape, bf), V(w_down.shape, bf),
           pltpu.SemaphoreType.DMA((2, 56 * chunks)), pltpu.SemaphoreType.DMA((4,))],
        compiler_params=pltpu.CompilerParams(collective_id=4, has_side_effects=True, vmem_limit_bytes=60 << 20),
        name="tail",
    )(partial.reshape(chunks, chans, size, width), gain.reshape(1, wide), bias.reshape(1, units), w_qkv, w_up, w_out, w_down)
    return out.reshape(tok, wide)


def on_device(
    chans,
    hids,
    pixels,
    patch_weight,
    channel_embed,
    pool_query,
    group_mix,
    assign,
    ln_gain,
    w_qkv,
    w_up,
    b_up,
    w_out,
    w_down,
):
    tok_count = pixels.shape[1]
    width_hid = patch_weight.shape[2]
    heads_dev = width_hid // HS
    partial_value = pool(pixels.shape[1], pixels, patch_weight, channel_embed, pool_query, group_mix, assign)
    tile = 16 * max(chans, hids)
    if chans == 4 and hids == 2 * chans and tok_count % tile == 0:
        chunks = 2 if tok_count % (2 * tile) == 0 else 1
        return tail(partial_value, ln_gain, b_up, w_qkv.transpose(1, 0, 2), w_up, w_out, w_down, chans, hids, chunks)
    normed_input, own_cols = layer_rows(partial_value, ln_gain, chans, hids)
    qkv_part = jnp.einsum("td,dke->kte", normed_input, w_qkv, preferred_element_type=jnp.float32)
    up_part = jnp.dot(normed_input, w_up, preferred_element_type=jnp.float32)
    qkv_rows, hidden = finish(
        qkv_part.astype(jnp.bfloat16), up_part.astype(jnp.bfloat16), b_up, heads_dev, chans, hids
    )
    images = tok_count // PATCHES
    queries, keys, values = qkv_rows.reshape(3, heads_dev, images, PATCHES, HS)
    scores = jnp.einsum("hbqe,hbke->hbqk", queries, keys, preferred_element_type=jnp.float32) * (
        2.0 / math.sqrt(HS)
    )
    expo = jnp.exp(scores)
    probs = (expo / jnp.sum(expo, axis=-1, keepdims=True)).astype(jnp.bfloat16)
    attended = jnp.einsum("hbqk,hbke->bqhe", probs, values, preferred_element_type=jnp.float32)
    attended = attended.astype(jnp.bfloat16).reshape(tok_count, width_hid)
    term = jnp.dot(attended, w_out, preferred_element_type=jnp.float32) + jnp.dot(
        hidden, w_down, preferred_element_type=jnp.float32
    )
    term = term.astype(jnp.bfloat16)
    if tok_count % (16 * hids) == 0:
        return total(term, own_cols, hids)
    mixed = lax.psum(term, "hid").astype(jnp.float32)
    return (own_cols.astype(jnp.float32) + mixed).astype(jnp.bfloat16)


def solution(mesh):
    in_specs = (
        P("chan", None, None),
        P("chan", None, "hid"),
        P("chan", "hid"),
        P("chan", "hid"),
        P("chan", "hid"),
        P("chan"),
        P("chan"),
        P("chan", None, "hid"),
        P("chan", "hid"),
        P("hid"),
        P("hid", "chan"),
        P("hid", "chan"),
    )
    out_specs = P(None, "chan")
    chans, hids = mesh.shape["chan"], mesh.shape["hid"]
    return jax.shard_map(
        functools.partial(on_device, chans, hids), mesh=mesh, in_specs=in_specs, out_specs=out_specs, check_vma=False
    )
```

```python
import functools
import math

import jax
import jax.numpy as jnp
from jax import lax
from jax.experimental import pallas as pl
from jax.experimental.pallas import tpu as pltpu
from jax.sharding import PartitionSpec as P

HS = 128
PATCHES = 256


epsilon = 1e-06


ACROSS = (((1,), (1,)), ((), ()))
LOG2E = math.log2(math.e)
SLOT = 16
ROWS = 256
CPS = 4
SLOTS = 3
VMEM_LIMIT = 63 << 20


def pool_setup(groups, size, query, mix, emb, quer, pick, shift, mixs, embs, fan):
    width = quer.shape[2]
    own = lax.broadcasted_iota(jnp.int32, (SLOT, width), 0) == lax.broadcasted_iota(jnp.int32, (SLOT, width), 1) // HS
    q = query[...].astype(jnp.float32)
    m = mix[...].astype(jnp.float32) * math.sqrt(0.5)
    pick[...] = jnp.where(own, 1.0, 0.0).astype(jnp.bfloat16)
    for g in range(groups):
        row = jnp.where(own, q[g:g+1, :], 0.0)
        quer[g] = row.astype(jnp.bfloat16)
        n = jnp.sqrt(jnp.sum(row * row, axis=1, keepdims=True)) * LOG2E
        shift[g] = jnp.broadcast_to(n, (SLOT, HS))
        mixs[g] = m[g:g+1]
    for c in range(0, emb.shape[0], 8):
        e = emb[c:c+8, :].astype(jnp.float32) * math.sqrt(0.5)
        for k in range(8):
            embs[c+k] = e[k:k+1]
    kind = lax.rem(lax.broadcasted_iota(jnp.int32, (HS, width), 0), HS // 2)
    head = lax.broadcasted_iota(jnp.int32, (HS, width), 1) // HS
    for j in range(size):
        fan[j] = jnp.where(kind == j * 8 + head, 1.0, 0.0).astype(jnp.bfloat16)

def features(tok, px_of, pw_of, bias, put):
    width = bias.shape[1]
    step = min(256, width)
    R = min(ROWS, tok)
    for n in range(width // step):
        cs = slice(n*step, (n+1)*step)
        for r in range(0, tok, R):
            e = jnp.dot(px_of(r, R), pw_of(cs), preferred_element_type=jnp.float32)
            u = e * math.sqrt(0.5) + bias[:, cs]
            g = (u * (1.0 + lax.erf(u))).astype(jnp.bfloat16)
            put(r, R, cs, g, g * g)

def weigh(tok, g, s, local, quer, pick, shift):
    dots = lax.dot_general(quer[local], g[...], ACROSS, preferred_element_type=jnp.float32)
    total = lax.dot_general(pick[...], s[...], ACROSS, preferred_element_type=jnp.float32)
    sh = jnp.concatenate([shift[local]] * (tok // HS), axis=1)
    score = dots * lax.rsqrt(total * (1.0 / HS) + 2 * epsilon) * (LOG2E / math.sqrt(HS))
    return jnp.exp2(score - sh)[0:8, :]

def weigh_pair(tok, g, s, first, second, quer, pick, shift):
    query = jnp.concatenate([quer[first], quer[second]], axis=0)
    dots = lax.dot_general(query, g[...], ACROSS, preferred_element_type=jnp.float32)
    total = lax.dot_general(pick[...], s[...], ACROSS, preferred_element_type=jnp.float32)[0:8]
    dots = jnp.concatenate([dots[0:8, :tok], dots[SLOT:SLOT + 8, tok:]], axis=1)
    sh = jnp.concatenate([shift[first][0:8]] * (tok // HS) + [shift[second][0:8]] * (tok // HS), axis=1)
    score = dots * lax.rsqrt(total * (1.0 / HS) + 2 * epsilon) * (LOG2E / math.sqrt(HS))
    return jnp.exp2(score - sh)

def merge(lo, hi, size, tok, order, feat, wts, mixs, fan, acc):
    width = feat.shape[2]
    step = min(256, width)
    def group(g, _):
        cs = [order[g*size + j] for j in range(size)]
        for b in range(0, tok, HS):
            bs = slice(b, b + HS)
            ws = [wts[c, :, bs] for c in cs]
            den = ws[0]
            for w in ws[1:]:
                den = den + w
            inv = 1.0 / den
            w = jnp.concatenate([w * inv for w in ws], axis=0)
            hi = w.astype(jnp.bfloat16).astype(jnp.float32)
            both = jnp.transpose(jnp.concatenate([hi, w - hi], axis=0))
            lhs = both.astype(jnp.bfloat16)
            for n in range(width // step):
                ns = slice(n*step, (n+1)*step)
                p = None
                for j in range(size):
                    t = jnp.dot(lhs, fan[j, :, ns], preferred_element_type=jnp.float32) * feat[cs[j], bs, ns].astype(jnp.float32)
                    p = t if p is None else p + t
                acc[bs, ns] += p * mixs[g, :, ns]
        return 0
    lax.fori_loop(lo, hi, group, 0)

def pool_kernel(groups, size, order, assign, pix, pw, emb, query, mix, out, feat, wts, acc, quer, pick, shift, mixs, embs, fan, g0, g1, s0, s1):
    t = pl.program_id(0); c = pl.program_id(1)
    tok = out.shape[0]
    gb, sb = (g0, g1), (s0, s1)
    @pl.when((t == 0) & (c == 0))
    def _():
        pool_setup(groups, size, query, mix, emb, quer, pick, shift, mixs, embs, fan)
    @pl.when(c == 0)
    def _():
        acc[...] = jnp.zeros_like(acc)
    def back(k):
        cc = c * CPS + k
        wts[cc] = weigh(tok, gb[k % 2], sb[k % 2], lax.rem(assign[cc], groups), quer, pick, shift)
    for k in range(CPS):
        cc = c * CPS + k
        def put(r, R, cs, g, s):
            feat[cc, r:r+R, cs] = g
            gb[k % 2][r:r+R, cs] = g
            sb[k % 2][r:r+R, cs] = s
        features(tok, lambda r, R: pix[k, r:r+R, :], lambda cs: pw[k, :, cs], embs[cc], put)
        if k: back(k - 1)
    back(CPS - 1)
    @pl.when(c == pl.num_programs(1)-1)
    def _():
        merge(0, groups, size, tok, order, feat, wts, mixs, fan, acc)
        out[...] = acc[...].astype(jnp.bfloat16)

def pool(T, pixels, patch_weight, channel_embed, pool_query, group_mix, assign):
    chans, tok, p2 = pixels.shape
    width = patch_weight.shape[2]
    groups = pool_query.shape[0]
    size = chans // groups
    idx = jnp.arange(chans, dtype=jnp.int32)
    key = assign * chans + idx
    rank = jnp.sum((key[None, :] < key[:, None]).astype(jnp.int32), axis=1)
    order = jnp.sum(jnp.where(rank[None, :] == idx[:, None], idx[None, :], 0), axis=1).astype(jnp.int32)
    full = lambda s: pl.BlockSpec(s, lambda t, c, *_: (0,)*len(s))
    vm = pltpu.VMEM
    spec = pltpu.PrefetchScalarGridSpec(num_scalar_prefetch=2, grid=(tok//T, chans//CPS),
        in_specs=[pl.BlockSpec((CPS,T,p2), lambda t,c,*_:(c,t,0)), pl.BlockSpec((CPS,p2,width), lambda t,c,*_:(c,0,0)),
          full((chans,width)), full((groups,width)), full((groups,width))],
        out_specs=pl.BlockSpec((T,width), lambda t,c,*_:(t,0)),
        scratch_shapes=[vm((chans,T,width), jnp.bfloat16), vm((chans,8,T), jnp.float32),
          vm((T,width), jnp.float32), vm((groups,SLOT,width), jnp.bfloat16), vm((SLOT,width), jnp.bfloat16),
          vm((groups,SLOT,HS), jnp.float32), vm((groups,1,width), jnp.float32), vm((chans,1,width), jnp.float32),
          vm((size,HS,width), jnp.bfloat16)] + [vm((T,width), jnp.bfloat16)]*4)
    return pl.pallas_call(functools.partial(pool_kernel, groups, size), grid_spec=spec, out_shape=jax.ShapeDtypeStruct((tok,width), jnp.bfloat16),
        compiler_params=pltpu.CompilerParams(dimension_semantics=("arbitrary","arbitrary"), vmem_limit_bytes=62<<20), name="pool")(
        order, assign, pixels, patch_weight, channel_embed, pool_query, group_mix)
def head_norm(values):
    return values * lax.rsqrt(jnp.mean(values * values, axis=-1, keepdims=True) + epsilon)


MESH = pl.DeviceIdType.MESH


def greet(peers):
    gate = pltpu.get_barrier_semaphore()
    for peer in peers:
        pl.semaphore_signal(gate, inc=1, device_id=peer, device_id_type=MESH)
    pl.semaphore_wait(gate, len(peers))


def send(src, dst, sems, slot, peer):
    copy = pltpu.make_async_remote_copy(
        src_ref=src, dst_ref=dst, send_sem=sems.at[0, slot], recv_sem=sems.at[1, slot],
        device_id=peer, device_id_type=MESH)
    copy.start()
    return copy


def places(chans, hids):
    a, b = lax.axis_index("chan"), lax.axis_index("hid")
    chips, chip, core = hids // 2, b // 2, b % 2
    rows = [{"chan": lax.rem(a + k, chans)} for k in range(1, chans)]
    far = [{"hid": lax.rem(chip + k, chips) * 2 + core} for k in range(1, chips)]
    return a, b, chips, chip, core, rows, far, {"hid": chip * 2 + (1 - core)}


def spread(src_of, slots, chips, chip, core, far, mate, away, near):
    sent = [send(src_of(chip * 2 + core), src_of(chip * 2 + core), away, k, peer) for k, peer in enumerate(far)]
    mine = src_of(chip * 2 + core)
    passed = [send(mine, mine, near, 0, mate)]
    for k in range(1, chips):
        sent[k - 1].wait_recv()
        piece = src_of(lax.rem(chip + chips - k, chips) * 2 + core)
        passed.append(send(piece, piece, near, k, mate))
    for copy in passed:
        copy.wait()
    for copy in sent:
        copy.wait_send()


def layer_kernel(chans, hids, part, gain, normed_ref, own_ref, parts, gath, stat, whole, stats, s1, s2, s3, s4, s5):
    a, b, chips, chip, core, rows, far, mate = places(chans, hids)
    greet(rows + far + [mate])
    width = part.shape[2]
    size = part.shape[1]
    copies = [send(part.at[lax.rem(a + k, chans)], parts.at[k - 1], s1, k - 1, rows[k - 1]) for k in range(1, chans)]
    total = part[a].astype(jnp.float32)
    for k in range(chans - 1):
        copies[k].wait_recv()
        total = total + parts[k].astype(jnp.float32)
    gath[b] = total.astype(jnp.bfloat16)
    spread(lambda i: gath.at[i], None, chips, chip, core, far, mate, s2, s3)
    first = jnp.zeros((size, 1), jnp.float32)
    second = jnp.zeros((size, 1), jnp.float32)
    for i in range(hids):
        x = gath[i].astype(jnp.float32)
        first = first + jnp.sum(x, axis=1, keepdims=True)
        second = second + jnp.sum(x * x, axis=1, keepdims=True)
    mean = first / (width * hids)
    scale = lax.rsqrt(second / (width * hids) - mean * mean + epsilon)
    stat[...] = jnp.where(lax.broadcasted_iota(jnp.int32, stat.shape, 1) == 0, mean, scale)
    ratio = hids // chans
    moved = []
    for k in range(1, chans):
        to = lax.rem(a + k, chans)
        moved.append(send(stat, stats.at[a], s5, k - 1, rows[k - 1]))
        moved.append(send(gath.at[pl.ds(to * ratio, ratio)], whole.at[a], s4, k - 1, rows[k - 1]))
    for copy in copies:
        copy.wait_send()

    def emit(i, x_of, st):
        for r in range(ratio):
            cs = slice(r * width, (r + 1) * width)
            x = x_of(r)
            own_ref[i, :, cs] = x
            normed_ref[i, :, cs] = (
                (x.astype(jnp.float32) - st[:, 0:1]) * st[:, 1:2] * gain[:, cs]
            ).astype(jnp.bfloat16)

    emit(a, lambda r: gath[a * ratio + r], stat[...])
    for copy in moved:
        copy.wait()
    for k in range(1, chans):
        i = lax.rem(a + k, chans)
        emit(i, lambda r: whole[i, r], stats[i])


def layer_rows(partial, gain, chans, hids):
    tok, width = partial.shape
    size = tok // chans
    wide = gain.shape[0]
    vm = pl.BlockSpec(memory_space=pltpu.VMEM)
    dma = pltpu.SemaphoreType.DMA
    shape = jax.ShapeDtypeStruct((chans, size, wide), jnp.bfloat16)
    normed, own = pl.pallas_call(
        functools.partial(layer_kernel, chans, hids), out_shape=(shape, shape), in_specs=[vm, vm], out_specs=(vm, vm),
        scratch_shapes=[
            pltpu.VMEM((chans - 1, size, width), jnp.bfloat16), pltpu.VMEM((hids, size, width), jnp.bfloat16),
            pltpu.VMEM((size, HS), jnp.float32), pltpu.VMEM((chans, hids // chans, size, width), jnp.bfloat16),
            pltpu.VMEM((chans, size, HS), jnp.float32),
            dma((2, chans - 1)), dma((2, hids // 2 - 1)), dma((2, hids // 2)), dma((2, chans - 1)), dma((2, chans - 1))],
        compiler_params=pltpu.CompilerParams(collective_id=1, has_side_effects=True, vmem_limit_bytes=40 << 20),
        name="layer_rows",
    )(partial.reshape(chans, size, width), gain.reshape(1, wide))
    return normed.reshape(tok, wide), own.reshape(tok, wide)


def finish_kernel(chans, hids, heads, qkv, up, bias, qkv_out, hid_out, qkv_in, up_in, s1, s2, s3, s4):
    a, rows = lax.axis_index("chan"), [{"chan": lax.rem(lax.axis_index("chan") + k, chans)} for k in range(1, chans)]
    greet(rows)
    got_q = [send(qkv.at[:, lax.rem(a + k, chans)], qkv_in.at[k - 1], s1, k - 1, rows[k - 1]) for k in range(1, chans)]
    got_u = [send(up.at[lax.rem(a + k, chans)], up_in.at[k - 1], s2, k - 1, rows[k - 1]) for k in range(1, chans)]
    for copy in got_q:
        copy.wait_recv()
    for h in range(3 * heads):
        kind, hs = h // heads, slice(h % heads * HS, (h % heads + 1) * HS)
        x = qkv[kind, a, :, hs].astype(jnp.float32)
        for k in range(chans - 1):
            x = x + qkv_in[k, kind, :, hs].astype(jnp.float32)
        if h < 2 * heads:
            x = x * lax.rsqrt(jnp.mean(x * x, axis=-1, keepdims=True) + epsilon)
        qkv_out[h, a] = x.astype(jnp.bfloat16)
    put_q = [send(qkv_out.at[:, a], qkv_out.at[:, a], s3, k, peer) for k, peer in enumerate(rows)]
    for copy in got_u:
        copy.wait_recv()
    step = HS
    for n in range(up.shape[2] // step):
        cs = slice(n * step, (n + 1) * step)
        x = up[a, :, cs].astype(jnp.float32)
        for k in range(chans - 1):
            x = x + up_in[k, :, cs].astype(jnp.float32)
        x = x + bias[:, cs]
        hid_out[a, :, cs] = ((0.5 * x) * (1.0 + lax.erf(x * math.sqrt(0.5)))).astype(jnp.bfloat16)
    put_u = [send(hid_out.at[a], hid_out.at[a], s4, k, peer) for k, peer in enumerate(rows)]
    for copy in got_q + got_u:
        copy.wait_send()
    for copy in put_q + put_u:
        copy.wait()


def finish(qkv, up, bias, heads, chans, hids):
    tok, wide = qkv.shape[1:]
    size, units = tok // chans, up.shape[1]
    vm = pl.BlockSpec(memory_space=pltpu.VMEM)
    dma = pltpu.SemaphoreType.DMA
    q, u = pl.pallas_call(
        functools.partial(finish_kernel, chans, hids, heads),
        out_shape=(jax.ShapeDtypeStruct((3 * heads, chans, size, HS), jnp.bfloat16), jax.ShapeDtypeStruct((chans, size, units), jnp.bfloat16)),
        in_specs=[vm] * 3, out_specs=(vm, vm),
        scratch_shapes=[
            pltpu.VMEM((chans - 1, 3, size, wide), jnp.bfloat16), pltpu.VMEM((chans - 1, size, units), jnp.bfloat16)]
        + [dma((2, chans - 1))] * 4,
        compiler_params=pltpu.CompilerParams(collective_id=2, has_side_effects=True, vmem_limit_bytes=40 << 20),
        name="finish",
    )(qkv.reshape(3, chans, size, wide), up.reshape(chans, size, units), bias.reshape(1, units))
    return q.reshape(3, heads, tok, HS), u.reshape(tok, units)


def total_kernel(hids, term, own, out, pair, half, pieces, s1, s2, s3, s4):
    b = lax.axis_index("hid")
    chips, chip, core = hids // 2, b // 2, b % 2
    far = [{"hid": lax.rem(chip + k, chips) * 2 + core} for k in range(1, chips)]
    mate = {"hid": chip * 2 + (1 - core)}
    greet(far + [mate])
    across = send(term.at[1 - core], pair, s1, 0, mate)
    across.wait_recv()
    for i in range(chips):
        half[i] = (term[core, i].astype(jnp.float32) + pair[i].astype(jnp.float32)).astype(jnp.bfloat16)
    copies = [send(half.at[lax.rem(chip + k, chips)], pieces.at[k - 1], s2, k - 1, far[k - 1]) for k in range(1, chips)]
    value = half[chip].astype(jnp.float32)
    for k in range(chips - 1):
        copies[k].wait_recv()
        value = value + pieces[k].astype(jnp.float32)
    out[core, chip] = (value + own[core, chip].astype(jnp.float32)).astype(jnp.bfloat16)
    spread(lambda i: out.at[i % 2, i // 2], None, chips, chip, core, far, mate, s3, s4)
    across.wait_send()
    for copy in copies:
        copy.wait_send()


def total(term, own, hids):
    tok, wide = term.shape
    chips, size = hids // 2, tok // hids
    vm = pl.BlockSpec(memory_space=pltpu.VMEM)
    dma = pltpu.SemaphoreType.DMA
    out = pl.pallas_call(
        functools.partial(total_kernel, hids),
        out_shape=jax.ShapeDtypeStruct((2, chips, size, wide), jnp.bfloat16), in_specs=[vm] * 2, out_specs=vm,
        scratch_shapes=[
            pltpu.VMEM((chips, size, wide), jnp.bfloat16), pltpu.VMEM((chips, size, wide), jnp.bfloat16),
            pltpu.VMEM((chips - 1, size, wide), jnp.bfloat16),
            dma((2, 1)), dma((2, chips - 1)), dma((2, chips - 1)), dma((2, chips))],
        compiler_params=pltpu.CompilerParams(collective_id=3, has_side_effects=True, vmem_limit_bytes=40 << 20),
        name="total",
    )(term.reshape(2, chips, size, wide), own.reshape(2, chips, size, wide))
    return out.reshape(tok, wide)


def column_steps(width, most=384):
    step = max(s for s in range(HS, most + 1, HS) if width % s == 0)
    return [slice(n, n + step) for n in range(0, width, step)]


class Tail:
    def __init__(self, chans, hids, refs):
        self.__dict__.update(refs)
        self.chans, self.hids = chans, hids
        self.a, self.b, self.chips, self.chip, self.core, self.rows, self.far, self.mate = places(chans, hids)
        self.y, self.x = self.a // 2, self.a % 2
        self.across_x, self.across_y = {"chan": self.y * 2 + 1 - self.x}, {"chan": (1 - self.y) * 2 + self.x}
        self.used, self.open = 0, []

    def put(self, src, dst, peer):
        slot = self.used
        self.used += 1
        copy = pltpu.make_async_remote_copy(
            src_ref=src, dst_ref=dst, send_sem=self.sems.at[0, slot], recv_sem=self.sems.at[1, slot],
            device_id=peer, device_id_type=MESH)
        copy.start()
        self.open.append(copy)
        return copy

    def drain(self):
        for copy in self.open:
            copy.wait_send()

    def scatter(self, t):
        a, chans = self.a, self.chans
        self.s_copies = getattr(self, "s_copies", {})
        self.s_copies[t] = [
            self.put(self.part.at[t, lax.rem(a + k, chans)], self.parts.at[t, k - 1], self.rows[k - 1]) for k in range(1, chans)]

    def collect(self, t):
        total = self.part[t, self.a].astype(jnp.float32)
        for k, copy in enumerate(self.s_copies[t]):
            copy.wait_recv()
            total = total + self.parts[t, k].astype(jnp.float32)
        b = self.b
        self.gath[t, b] = total.astype(jnp.bfloat16)
        mine = self.gath.at[t, b]
        self.g_far = getattr(self, "g_far", {})
        self.g_near = getattr(self, "g_near", {})
        self.g_far[t] = [self.put(mine, mine, peer) for peer in self.far]
        self.g_near[t] = [self.put(mine, mine, self.mate)]

    def relay(self, t):
        self.c_piece = getattr(self, "c_piece", {})
        a, chans = self.a, self.chans
        for k in range(1, self.chips):
            self.g_far[t][k - 1].wait_recv()
            piece = self.gath.at[t, lax.rem(self.chip + self.chips - k, self.chips) * 2 + self.core]
            self.g_near[t].append(self.put(piece, piece, self.mate))
        self.c_piece[t] = [
            self.put(self.gath.at[t, lax.rem(a + k, chans) * 2 + self.core], self.whole.at[t, a, self.core], self.rows[k - 1])
            for k in range(1, chans)]

    def exchange(self, t):
        for copy in self.g_near[t]:
            copy.wait_recv()
        size, width = self.gath.shape[2:]
        first = jnp.zeros((size, 1), jnp.float32)
        second = jnp.zeros((size, 1), jnp.float32)
        for i in range(self.hids):
            x = self.gath[t, i].astype(jnp.float32)
            first = first + jnp.sum(x, axis=1, keepdims=True)
            second = second + jnp.sum(x * x, axis=1, keepdims=True)
        mean = first / (width * self.hids)
        scale = lax.rsqrt(second / (width * self.hids) - mean * mean + epsilon)
        self.stat[t] = jnp.where(lax.broadcasted_iota(jnp.int32, (size, HS), 1) == 0, mean, scale)
        self.c_stat = getattr(self, "c_stat", {})
        a, chans = self.a, self.chans
        self.c_stat[t] = [self.put(self.stat.at[t], self.stats.at[t, a], peer) for peer in self.rows]

    def share(self, t):
        self.c_near = getattr(self, "c_near", {})
        self.c_near[t] = []
        for k in range(1, self.chans):
            self.c_piece[t][k - 1].wait_recv()
            piece = self.whole.at[t, lax.rem(self.a + self.chans - k, self.chans), self.core]
            self.c_near[t].append(self.put(piece, piece, self.mate))

    def norm(self, t):
        size, width = self.gath.shape[2:]

        def emit(i, x_of, st):
            for r in range(2):
                self.own[t, i, :, r * width:(r + 1) * width] = x_of(r)

            def column(n, _):
                cs = pl.ds(pl.multiple_of(n * HS, HS), HS)
                x = self.own[t, i, :, cs].astype(jnp.float32)
                self.normed[t, i, :, cs] = (
                    (x - st[:, 0:1]) * st[:, 1:2] * self.gain[pl.ds(n, 1), :]).astype(jnp.bfloat16)
                return 0
            lax.fori_loop(0, 2 * width // HS, column, 0, unroll=2)

        emit(self.a, lambda r: self.gath[t, self.a * 2 + r], self.stat[t])
        for copy in self.c_stat[t] + self.c_near[t]:
            copy.wait_recv()
        for k in range(1, self.chans):
            i = lax.rem(self.a + k, self.chans)
            emit(i, lambda r: self.whole[t, i, r], self.stats[t, i])

    def multiply(self, t, kind):
        buf, weights = self.units[kind][0], self.units[kind][4]
        size = buf.shape[3]
        wide = buf.shape[4]
        step = min(256, self.w_qkv.shape[2])
        x = self.normed[t].reshape(4 * size, self.normed.shape[3])
        per = weights.shape[-1]

        for k in range(wide // per):
            def tile(n, _):
                off = pl.multiple_of(n * step, step)
                w = weights[k, :, pl.ds(off, step)] if kind == "qkv" else weights[:, pl.ds(off, step)]
                e = jnp.dot(x, w, preferred_element_type=jnp.float32).astype(jnp.bfloat16)
                buf[t, :, :, :, pl.ds(pl.multiple_of(k * per + off, step), step)] = e.reshape(2, 2, size, step)
                return 0
            lax.fori_loop(0, per // step, tile, 0)

    def halves(self, kind):
        wide = self.units[kind][0].shape[4]
        return slice(0, wide // 2), slice(wide // 2, wide)

    def reduce1(self, t, kind):
        buf, got1 = self.units[kind][:2]
        left, right = self.halves(kind)
        self.d1 = getattr(self, "d1", {})
        self.d1[t, kind] = (
            self.put(buf.at[t, :, 1 - self.x, :, left], got1.at[t, 0], self.across_x),
            self.put(buf.at[t, 1 - self.y, :, :, right], got1.at[t, 1], self.across_y))

    def reduce2(self, t, kind):
        buf, got1, mid, got2 = self.units[kind][:4]
        left, right = self.halves(kind)
        self.d2 = getattr(self, "d2", {})
        for copy in self.d1[t, kind]:
            copy.wait_recv()
        for side in range(2):
            base = (left, right)[side].start
            for cs in column_steps(got1.shape[4]):
                here = slice(base + cs.start, base + cs.stop)
                mine = buf[t, 1 - self.y, self.x, :, here] if side == 0 else buf[t, self.y, 1 - self.x, :, here]
                got = got1[t, 0, 1 - self.y, :, cs] if side == 0 else got1[t, 1, 1 - self.x, :, cs]
                mid[t, side, :, cs] = (mine.astype(jnp.float32) + got.astype(jnp.float32)).astype(jnp.bfloat16)
            self.d2[t, kind, side] = self.put(mid.at[t, side], got2.at[t, side], (self.across_y, self.across_x)[side])

    def act(self, t, kind):
        buf, got1, _, got2, _, full = self.units[kind]
        left, right = self.halves(kind)
        self.e1 = getattr(self, "e1", {})
        rotated = 2 * self.w_qkv.shape[2]
        for side in range(2):
            self.d2[t, kind, side].wait_recv()
            base = (left, right)[side].start
            for c in range(0, got1.shape[4], HS):
                cs = slice(c, c + HS)
                here = slice(base + c, base + c + HS)
                v = buf[t, self.y, self.x, :, here].astype(jnp.float32) + got2[t, side, :, cs].astype(jnp.float32)
                v = v + (got1[t, 0, self.y, :, cs] if side == 0 else got1[t, 1, self.x, :, cs]).astype(jnp.float32)
                if kind == "up":
                    v = v + self.bias[(base + c) // HS:(base + c) // HS + 1, :]
                    v = (0.5 * v) * (1.0 + lax.erf(v * math.sqrt(0.5)))
                elif base + c < rotated:
                    v = v * lax.rsqrt(jnp.mean(v * v, axis=-1, keepdims=True) + epsilon)
                full[t, self.y, self.x, :, here] = v.astype(jnp.bfloat16)
            mine = full.at[t, self.y, self.x, :, (left, right)[side]]
            self.e1[t, kind, side] = self.put(mine, mine, (self.across_y, self.across_x)[side])

    def gather2(self, t, kind):
        full = self.units[kind][5]
        left, right = self.halves(kind)
        self.e2 = getattr(self, "e2", {})
        for side in range(2):
            self.e1[t, kind, side].wait_recv()
            mine = full.at[t, :, self.x, :, left] if side == 0 else full.at[t, self.y, :, :, right]
            self.e2[t, kind, side] = self.put(mine, mine, (self.across_x, self.across_y)[side])

    def whole_unit(self, t, kind):
        for side in range(2):
            self.e2[t, kind, side].wait_recv()

    def attend(self, chunks, share, shares):
        full = self.units["qkv"][5]
        size = full.shape[3]
        wide = self.w_qkv.shape[2]
        tok = chunks * 4 * size

        def head(h, _):
            def take(kind):
                cs = pl.ds(pl.multiple_of(kind * wide + h * HS, HS), HS)
                return full[:, :, :, :, cs].reshape(tok, HS)
            q, k, v = take(0), take(1), take(2)
            for r in range(0, tok, PATCHES):
                rs = slice(r, r + PATCHES)
                scores = lax.dot_general(q[rs], k[rs], ACROSS, preferred_element_type=jnp.float32) * (2.0 / math.sqrt(HS))
                expo = jnp.exp(scores)
                probs = (expo * (1.0 / jnp.sum(expo, axis=-1, keepdims=True))).astype(jnp.bfloat16)
                got = jnp.dot(probs, v[rs], preferred_element_type=jnp.float32).astype(jnp.bfloat16)
                self.attended[rs, pl.ds(pl.multiple_of(h * HS, HS), HS)] = got
            return 0

        heads = wide // HS
        lax.fori_loop(heads * share // shares, heads * (share + 1) // shares, head, 0)

    def fetch_down(self):
        width = self.feat.shape[2]
        nd, no = self.wd_hbm.shape[0], self.wo_hbm.shape[0]
        self.down_loads = []
        for side in range(2):
            cs = slice(side * width, (side + 1) * width)
            for hbm, at, count in ((self.wd_hbm, side * nd, nd), (self.wo_hbm, 2 * nd + side * no, no)):
                copy = pltpu.make_async_copy(hbm.at[:, :, cs], self.feat.at[at:at + count], self.loads.at[2 + len(self.down_loads)])
                copy.start()
                self.down_loads.append(copy)

    def down(self, t):
        full = self.units["up"][5]
        size = full.shape[3]
        rows = 4 * size
        width = self.feat.shape[2]
        step = min(256, width)
        nd, no = self.wd_hbm.shape[0], self.wo_hbm.shape[0]
        deep = self.feat.shape[1]
        hidden = full[t].reshape(rows, full.shape[4])
        att = self.attended[t * rows:(t + 1) * rows]

        for side in range(2):
            def tile(n, _):
                off = pl.multiple_of(n * step, step)
                cs = pl.ds(off, step)
                wd = self.feat[side * nd:(side + 1) * nd, :, cs].reshape(nd * deep, step)
                wo = self.feat[2 * nd + side * no:2 * nd + (side + 1) * no, :, cs].reshape(no * deep, step)
                e = jnp.dot(hidden, wd, preferred_element_type=jnp.float32) + jnp.dot(att, wo, preferred_element_type=jnp.float32)
                to = pl.ds(pl.multiple_of(side * width + off, step), step)
                self.term[t, :, :, :, to] = e.astype(jnp.bfloat16).reshape(2, self.chips, rows // self.hids, step)
                return 0
            lax.fori_loop(0, width // step, tile, 0)
        self.f1 = getattr(self, "f1", {})
        self.f1[t] = self.put(self.term.at[t, 1 - self.core], self.pair.at[t], self.mate)

    def total1(self, t):
        self.f1[t].wait_recv()
        self.f2 = getattr(self, "f2", {})
        chips, chip = self.chips, self.chip
        for i in range(chips):
            self.half[t, i] = (
                self.term[t, self.core, i].astype(jnp.float32) + self.pair[t, i].astype(jnp.float32)).astype(jnp.bfloat16)
        self.f2[t] = [
            self.put(self.half.at[t, lax.rem(chip + k, chips)], self.pieces.at[t, k - 1], self.far[k - 1]) for k in range(1, chips)]

    def total2(self, t):
        value = self.half[t, self.chip].astype(jnp.float32)
        for k, copy in enumerate(self.f2[t]):
            copy.wait_recv()
            value = value + self.pieces[t, k].astype(jnp.float32)
        core, chip, chips = self.core, self.chip, self.chips
        own = self.own_rows(t)
        self.out[t, core, chip] = (value + own).astype(jnp.bfloat16)
        mine = self.out.at[t, core, chip]
        self.f3 = getattr(self, "f3", {})
        self.f4 = getattr(self, "f4", {})
        self.f3[t] = [self.put(mine, mine, peer) for peer in self.far]
        self.f4[t] = [self.put(mine, mine, self.mate)]

    def own_rows(self, t):
        rows = self.out.shape[3]
        place = (self.core * self.chips + self.chip) * rows
        size = self.own.shape[2]
        return self.own[t, place // size, pl.ds(pl.multiple_of(lax.rem(place, size), rows), rows), :].astype(jnp.float32)

    def total3(self, t):
        for k in range(1, self.chips):
            self.f3[t][k - 1].wait_recv()
            piece = self.out.at[t, self.core, lax.rem(self.chip + self.chips - k, self.chips)]
            self.f4[t].append(self.put(piece, piece, self.mate))

    def total4(self, t):
        for copy in self.f4[t]:
            copy.wait_recv()


NAMES = [
    "order", "assign", "emb", "query", "mix", "gain", "bias", "pix_hbm", "pw_hbm", "wq_hbm", "wu_hbm", "wo_hbm", "wd_hbm", "out",
    "part", "parts", "gath", "stat", "stats", "whole", "own", "normed", "q0", "q1", "q2", "q3", "q4", "u0",
    "u1", "u2", "u3", "u4", "attended", "term", "pair", "half", "pieces", "w_qkv", "w_up", "feat", "wts", "acc",
    "quer", "pick", "shift", "mixs", "embs", "fan", "g0", "g1", "s0", "s1", "pix", "pw", "sems", "loads",
    "fetches",
]


def block_kernel(chans, hids, chunks, groups, *refs):
    r = dict(zip(NAMES, refs))
    r["units"] = {
        "qkv": [r["q0"], r["q1"], r["q2"], r["q3"], r["w_qkv"], r["q4"]],
        "up": [r["u0"], r["u1"], r["u2"], r["u3"], r["w_up"], r["u4"]]}
    s = Tail(chans, hids, r)
    count, tok = s.feat.shape[:2]
    size = count // groups
    slots, per = s.pix.shape[:2]
    blocks = count // per
    ahead = slots - 1
    gb, sb = (s.g0, s.g1), (s.s0, s.s1)

    def fetch(t, i):
        slot = lax.rem(t * blocks + i, slots)
        cs = pl.ds(i * per, per)
        return (pltpu.make_async_copy(s.pw_hbm.at[cs], s.pw.at[slot], s.fetches.at[0, slot]),
                pltpu.make_async_copy(s.pix_hbm.at[cs, t * tok:(t + 1) * tok], s.pix.at[slot], s.fetches.at[1, slot]))

    def start(t, i):
        for copy in fetch(t, i):
            copy.start()

    def back(cc, pair):
        w = weigh_pair(tok, gb[pair], sb[pair], s.assign[cc], s.assign[cc + 1], s.quer, s.pick, s.shift)
        s.wts[cc] = w[:, :tok]
        s.wts[cc + 1] = w[:, tok:]

    def embed(t, lo, hi):
        def block(i, _):
            @pl.when(i + ahead < blocks)
            def _():
                start(t, i + ahead)
            if t + 1 < chunks:
                @pl.when(i + ahead >= blocks)
                def _():
                    start(t + 1, i + ahead - blocks)
            for copy in fetch(t, i):
                copy.wait()
            slot = lax.rem(t * blocks + i, slots)

            for k in range(per):
                cc = i * per + k
                pair = k // 2 % 2
                def keep(rr, R, cs, g, sq):
                    s.feat[cc, rr:rr+R, cs] = g
                    at = k % 2 * tok + rr
                    gb[pair][at:at+R, cs] = g
                    sb[pair][at:at+R, cs] = sq
                features(tok, lambda rr, R: s.pix[slot, k, rr:rr+R, :], lambda cs: s.pw[slot, k, :, cs], s.embs[cc], keep)
                if k % 2:
                    back(jnp.maximum(cc - 3, 0), 1 - pair)
            return 0
        lax.fori_loop(lo, hi, block, 0)
        if hi == blocks:
            back(count - 2, 1)

    def mix_in(t, lo, hi):
        if lo == 0:
            s.acc[...] = jnp.zeros_like(s.acc)
        merge(lo, hi, size, tok, s.order, s.feat, s.wts, s.mixs, s.fan, s.acc)
        if hi == groups:
            s.part[t] = s.acc[...].astype(jnp.bfloat16).reshape(s.part.shape[1:])

    gate = pltpu.get_barrier_semaphore()
    peers = s.rows + s.far + [s.mate]
    for peer in peers:
        pl.semaphore_signal(gate, inc=1, device_id=peer, device_id_type=MESH)
    for i in range(ahead):
        start(0, i)
    loads = [pltpu.make_async_copy(s.wq_hbm, s.w_qkv, s.loads.at[0]), pltpu.make_async_copy(s.wu_hbm, s.w_up, s.loads.at[1])]
    pool_setup(groups, size, s.query, s.mix, s.emb, s.quer, s.pick, s.shift, s.mixs, s.embs, s.fan)
    embed(0, 0, blocks // 3)
    loads[0].start()
    embed(0, blocks // 3, 2 * blocks // 3)
    loads[1].start()
    embed(0, 2 * blocks // 3, blocks)
    mix_in(0, 0, groups)
    pl.semaphore_wait(gate, len(peers))
    s.scatter(0)

    def front(t):
        if t == 0:
            loads[0].wait()
        s.norm(t)
        s.multiply(t, "qkv")
        s.reduce1(t, "qkv")
        if t == 0:
            loads[1].wait()
        s.multiply(t, "up")
        s.reduce1(t, "up")

    for t in range(1, chunks):
        u = t - 1
        steps = [(4, lambda: s.collect(u)), (9, lambda: s.relay(u)), (11, lambda: s.exchange(u)), (13, lambda: s.share(u)),
                 (15, lambda: front(u)), (19, lambda: s.reduce2(u, "qkv")), (22, lambda: s.reduce2(u, "up"))]
        at = 0
        for mark, step in steps:
            mark = min(blocks, mark * blocks // 24)
            if mark > at:
                embed(t, at, mark)
            at = mark
            step()
        if at < blocks:
            embed(t, at, blocks)
        cuts = [groups * k // 4 for k in range(5)]
        mix_in(t, cuts[0], cuts[1])
        s.act(u, "qkv")
        mix_in(t, cuts[1], cuts[2])
        s.act(u, "up")
        mix_in(t, cuts[2], cuts[3])
        s.gather2(u, "qkv")
        mix_in(t, cuts[3], cuts[4])
        s.scatter(t)
        s.gather2(u, "up")
    s.fetch_down()
    last = chunks - 1
    s.collect(last)
    s.relay(last)
    s.exchange(last)
    s.share(last)
    front(last)
    s.reduce2(last, "qkv")
    s.act(last, "qkv")
    s.reduce2(last, "up")
    s.gather2(last, "qkv")
    s.act(last, "up")
    every = range(chunks)
    for t in every:
        s.whole_unit(t, "qkv")
    s.attend(chunks, 0, 3)
    s.gather2(last, "up")
    s.attend(chunks, 1, 3)
    s.attend(chunks, 2, 3)
    for copy in s.down_loads:
        copy.wait()
    for t in every:
        s.whole_unit(t, "up")
        if t:
            s.total1(t - 1)
        s.down(t)
    s.total1(last)
    for step in (s.total2, s.total3, s.total4):
        for t in every:
            step(t)
    s.drain()


def sort_channels(assign):
    chans = assign.shape[0]
    idx = jnp.arange(chans, dtype=jnp.int32)
    key = assign * chans + idx
    rank = jnp.sum((key[None, :] < key[:, None]).astype(jnp.int32), axis=1)
    return jnp.sum(jnp.where(rank[None, :] == idx[:, None], idx[None, :], 0), axis=1).astype(jnp.int32)


def block(pixels, patch_weight, channel_embed, pool_query, group_mix, assign, gain, bias, w_qkv, w_up, w_out, w_down, chans, hids, chunks):
    count, tok, p2 = pixels.shape
    width = patch_weight.shape[2]
    groups = pool_query.shape[0]
    rows = tok // chunks
    size = rows // chans
    wide = gain.shape[0]
    chips = hids // 2
    qw, units = w_qkv.shape[0] * w_qkv.shape[2], w_up.shape[1]
    bf, f32 = jnp.bfloat16, jnp.float32
    sm = pl.BlockSpec(memory_space=pltpu.SMEM)
    vm, hbm = pl.BlockSpec(memory_space=pltpu.VMEM), pl.BlockSpec(memory_space=pl.ANY)
    V = pltpu.VMEM

    def unit(w):
        return [V((chunks, 2, 2, size, w), bf), V((chunks, 2, 2, size, w // 2), bf), V((chunks, 2, size, w // 2), bf),
                V((chunks, 2, size, w // 2), bf), V((chunks, 2, 2, size, w), bf)]

    few = rows // hids
    out = pl.pallas_call(
        functools.partial(block_kernel, chans, hids, chunks, groups),
        out_shape=jax.ShapeDtypeStruct((chunks, 2, chips, few, wide), bf),
        in_specs=[sm] * 2 + [vm] * 5 + [hbm] * 6, out_specs=vm,
        scratch_shapes=[
            V((chunks, chans, size, width), bf),
            V((chunks, chans - 1, size, width), bf), V((chunks, hids, size, width), bf), V((chunks, size, HS), f32),
            V((chunks, chans, size, HS), f32), V((chunks, chans, 2, size, width), bf),
            V((chunks, chans, size, wide), bf), V((chunks, chans, size, wide), bf)]
        + unit(qw) + unit(units)
        + [V((tok, w_out.shape[0]), bf), V((chunks, 2, chips, few, wide), bf), V((chunks, chips, few, wide), bf),
           V((chunks, chips, few, wide), bf), V((chunks, chips - 1, few, wide), bf),
           V(w_qkv.shape, bf), V(w_up.shape, bf),
           V((count, rows, width), bf), V((count, 8, rows), f32), V((rows, width), f32),
           V((groups, SLOT, width), bf), V((SLOT, width), bf), V((groups, SLOT, HS), f32),
           V((groups, 1, width), f32), V((count, 1, width), f32), V((count // groups, HS, width), bf)]
        + [V((2 * rows, width), bf)] * 4
        + [V((SLOTS, CPS, rows, p2), bf), V((SLOTS, CPS, p2, width), bf),
           pltpu.SemaphoreType.DMA((2, 48 * chunks)), pltpu.SemaphoreType.DMA((6,)), pltpu.SemaphoreType.DMA((2, SLOTS))],
        compiler_params=pltpu.CompilerParams(collective_id=4, has_side_effects=True, vmem_limit_bytes=VMEM_LIMIT),
        name="block",
    )(sort_channels(assign), lax.rem(assign, groups), channel_embed, pool_query, group_mix, gain.reshape(wide // HS, HS), bias.reshape(units // HS, HS),
      pixels, patch_weight, w_qkv, w_up, w_out.reshape(w_out.shape[0] // rows, rows, wide), w_down.reshape(units // rows, rows, wide))
    return out.reshape(tok, wide)


def on_device(
    chans,
    hids,
    pixels,
    patch_weight,
    channel_embed,
    pool_query,
    group_mix,
    assign,
    ln_gain,
    w_qkv,
    w_up,
    b_up,
    w_out,
    w_down,
):
    tok_count = pixels.shape[1]
    width_hid = patch_weight.shape[2]
    heads_dev = width_hid // HS
    tile = 16 * max(chans, hids)
    chunks = 2 if tok_count % (2 * tile) == 0 else 1
    rows = tok_count // chunks
    units = w_up.shape[1]
    room = 2 * (units + width_hid) <= pixels.shape[0] * rows
    if chans == 4 and hids == 2 * chans and tok_count % tile == 0 and rows % HS == 0 and units % rows == 0 and width_hid % rows == 0 and room:
        return block(pixels, patch_weight, channel_embed, pool_query, group_mix, assign, ln_gain, b_up,
                     w_qkv.transpose(1, 0, 2), w_up, w_out, w_down, chans, hids, chunks)
    partial_value = pool(tok_count, pixels, patch_weight, channel_embed, pool_query, group_mix, assign)
    normed_input, own_cols = layer_rows(partial_value, ln_gain, chans, hids)
    qkv_part = jnp.einsum("td,dke->kte", normed_input, w_qkv, preferred_element_type=jnp.float32)
    up_part = jnp.dot(normed_input, w_up, preferred_element_type=jnp.float32)
    qkv_rows, hidden = finish(
        qkv_part.astype(jnp.bfloat16), up_part.astype(jnp.bfloat16), b_up, heads_dev, chans, hids
    )
    images = tok_count // PATCHES
    queries, keys, values = qkv_rows.reshape(3, heads_dev, images, PATCHES, HS)
    scores = jnp.einsum("hbqe,hbke->hbqk", queries, keys, preferred_element_type=jnp.float32) * (
        2.0 / math.sqrt(HS)
    )
    expo = jnp.exp(scores)
    probs = (expo / jnp.sum(expo, axis=-1, keepdims=True)).astype(jnp.bfloat16)
    attended = jnp.einsum("hbqk,hbke->bqhe", probs, values, preferred_element_type=jnp.float32)
    attended = attended.astype(jnp.bfloat16).reshape(tok_count, width_hid)
    term = jnp.dot(attended, w_out, preferred_element_type=jnp.float32) + jnp.dot(
        hidden, w_down, preferred_element_type=jnp.float32
    )
    term = term.astype(jnp.bfloat16)
    if tok_count % (16 * hids) == 0:
        return total(term, own_cols, hids)
    mixed = lax.psum(term, "hid").astype(jnp.float32)
    return (own_cols.astype(jnp.float32) + mixed).astype(jnp.bfloat16)


def solution(mesh):
    in_specs = (
        P("chan", None, None),
        P("chan", None, "hid"),
        P("chan", "hid"),
        P("chan", "hid"),
        P("chan", "hid"),
        P("chan"),
        P("chan"),
        P("chan", None, "hid"),
        P("chan", "hid"),
        P("hid"),
        P("hid", "chan"),
        P("hid", "chan"),
    )
    out_specs = P(None, "chan")
    chans, hids = mesh.shape["chan"], mesh.shape["hid"]
    return jax.shard_map(
        functools.partial(on_device, chans, hids), mesh=mesh, in_specs=in_specs, out_specs=out_specs, check_vma=False
    )
```
